32 devices in a mesh: grp: 4 (over y, x), shard: 8 (over z, core).
Axes of the slice: x: 2, y: 2, z: 4, core: 2. Of those that a mesh axis runs over, the one named last changes fastest.
Arguments:
- queries: bfloat16 [16, 32, 128], P('grp', 'shard'), may hold values from -7 to 7
- paged_key_cache: bfloat16 [2048, 8, 64, 128], P(('grp', 'shard')), may hold values from -8 to 8
- paged_value_cache: bfloat16 [2048, 8, 64, 128], P(('grp', 'shard')), may hold values from -6 to 6
- summary_keys: bfloat16 [8, 2048, 128], P(None, ('grp', 'shard')), may hold values from -8 to 8
- summary_values: bfloat16 [8, 2048, 128], P(None, ('grp', 'shard')), may hold values from -6 to 6
- gate_logits: float32 [2, 16, 32], P(None, 'grp', 'shard'), may hold values from -6 to 6
- block_group_row: int32 [16, 128], P('grp'), may hold values from 0 to 511, as said below
- picked: int32 [8, 16, 8], P(None, 'grp'), may hold values from 0 to 127, as said below
Outputs:
- attention: float32 [16, 32, 128], P('grp', 'shard')
- retrieval_counts: float32 [128], replicated
The draws below stay inside these ranges and needn't reach their ends.
Inputs may be any that keep to these rules, and one draw needn't show every extreme that they name: block_group_row is one to one within each group. For slot = block_group_row[b, k], slot // 64 is the index along shard of the device that stores block k of sequence b and slot % 64 its place there; every device stores 16 blocks of each sequence of its group, the sequence numbered s within the group in places s * 16 to s * 16 + 15. picked[g, b, :] names 8 blocks of sequence b stored on 8 different devices. For one key head and one group, take an aligned run of r sequences of the group (r dividing 4): among all their picks at most min(r, 8) are stored on any one device; for r = 4 some device stores exactly min(4, 8) of them.
All inputs are finite; a program needn't handle non-finite values.
Results may differ from the reference program's by a relative error of at most 0.006.
Values may be sent and summed in bfloat16 or wider, within the bound.
No kernel may reach another device: no remote copies, remote signals or barrier semaphores. Data moves between devices by JAX's collectives and lax.ppermute only.
A program may use at most 128 MiB of HBM per device.

```python
import jax
import jax.numpy as jnp
from jax import lax

HQ = 32
KEY_HEADS = 8
HEAD_SIZE = 128
QUERY_PER_KEY = 4
BLOCK_TOKENS = 64
PICKED_BLOCKS = 8
SEQ_GRP = 4
BPO = 16
BLK_DEV = 64
SEQUENCE_BLOCKS = 128
SLOTS_GRP = 512
TOTAL_BLOCKS = 2048
SEQUENCE_TOTAL = 16


def layout(key):
    partition_count = SEQUENCE_BLOCKS // BPO
    group_number = SEQUENCE_TOTAL // SEQ_GRP
    key_place, key_heat, key_sorting, key_depth = jax.random.split(jax.random.fold_in(key, 4242), 4)
    placement = jax.vmap(lambda subkey: jax.random.permutation(subkey, SEQUENCE_BLOCKS))(jax.random.split(key_place, SEQUENCE_TOTAL)).astype(jnp.int32)
    owners = placement % partition_count
    depth = placement // partition_count
    within = (jnp.arange(SEQUENCE_TOTAL, dtype=jnp.int32) % SEQ_GRP)[:, None]
    block_group_row = owners * BLK_DEV + within * BPO + depth
    reverse_order = jnp.argsort(placement, axis=1).astype(jnp.int32)
    heated = (jax.random.randint(key_heat, (group_number, partition_count), 0, 4) == 0).astype(jnp.int32)
    score_ranking = jax.random.randint(key_sorting, (KEY_HEADS, group_number, partition_count), 0, 1024)
    scoring = (heated[None] * 1024 + score_ranking) * partition_count + jnp.arange(partition_count, dtype=jnp.int32)
    ordering = jnp.argsort(-scoring, axis=-1).astype(jnp.int32)
    window = (jnp.arange(SEQ_GRP)[:, None] + jnp.arange(PICKED_BLOCKS)[None, :]) % partition_count
    picked_holder = ordering[:, :, window]
    picked_level = jax.random.randint(key_depth, picked_holder.shape, 0, BPO)
    requested_rows = (picked_level * partition_count + picked_holder).reshape(KEY_HEADS, SEQUENCE_TOTAL, PICKED_BLOCKS).astype(jnp.int32)
    picked = jnp.take_along_axis(jnp.broadcast_to(reverse_order[None], (KEY_HEADS, SEQUENCE_TOTAL, SEQUENCE_BLOCKS)), requested_rows, axis=2)
    return (block_group_row.astype(jnp.int32), picked.astype(jnp.int32))


def draw_queries(key, part):
    start_offset = jnp.clip(jax.random.normal(jax.random.fold_in(key, 11), (SEQUENCE_TOTAL, HQ, HEAD_SIZE), jnp.float32), -6.0, 6.0)
    return start_offset.astype(jnp.bfloat16)


def draw_paged_key_cache(key, part):
    start_offset = jnp.clip(2.0 * jax.random.normal(jax.random.fold_in(key, 21), (TOTAL_BLOCKS, KEY_HEADS, BLOCK_TOKENS, HEAD_SIZE), jnp.float32), -8.0, 8.0)
    return start_offset.astype(jnp.bfloat16)


def draw_summary_keys(key, part):
    start_offset = jnp.clip(2.0 * jax.random.normal(jax.random.fold_in(key, 41), (KEY_HEADS, TOTAL_BLOCKS, HEAD_SIZE), jnp.float32), -8.0, 8.0)
    return start_offset.astype(jnp.bfloat16)


def draw_block_group_row(key, part):
    return layout(key)[0]


def draw_picked(key, part):
    return layout(key)[1]


def block_levels(rng, dims, shards, low, largest):
    def one(dim, parts):
        heights = jax.random.uniform(jax.random.fold_in(jax.random.fold_in(rng, 6), dim), (parts,), jnp.float32, low / len(shards), largest / len(shards))
        return jnp.repeat(jnp.exp(heights), dims[dim] // parts).reshape((-1,) + (1,) * (len(dims) - dim - 1))

    level = one(*shards[0])
    for cut in shards[1:]:
        level = level * one(*cut)
    return level


def bell_draw(key, dims, width, reach, cuts=(), kind=jnp.bfloat16):
    entries = jax.random.normal(key, dims, jnp.float32) * width
    if len(cuts) > 0:
        entries = block_levels(key, dims, cuts, -0.22, 0.18) * entries
    return jnp.clip(entries, min=-reach, max=reach).astype(kind)


def setup_inputs(seed: int = 0) -> dict:
    splits = jax.random.split(jax.random.key(seed), 9)
    return {
        "queries": draw_queries(jax.random.fold_in(splits[8], 71), 0),
        "paged_key_cache": draw_paged_key_cache(jax.random.fold_in(splits[8], 71), 0),
        "paged_value_cache": bell_draw(splits[2], (TOTAL_BLOCKS, KEY_HEADS, BLOCK_TOKENS, HEAD_SIZE), 1.0, 6.0, ((0, 32),)),
        "summary_keys": draw_summary_keys(jax.random.fold_in(splits[8], 71), 0),
        "summary_values": bell_draw(splits[4], (KEY_HEADS, TOTAL_BLOCKS, HEAD_SIZE), 1.0, 6.0, ((1, 32),)),
        "gate_logits": bell_draw(splits[5], (2, SEQUENCE_TOTAL, HQ), 1.5, 6.0, ((1, 4), (2, 8)), jnp.float32),
        "block_group_row": draw_block_group_row(jax.random.fold_in(splits[8], 71), 0),
        "picked": draw_picked(jax.random.fold_in(splits[8], 71), 0),
    }


def attend(query_rows, key_rows, value_rows):
    scaling = query_rows.shape[-1] ** -0.5
    scores = jnp.einsum("rhd,rnd->rhn", query_rows.astype(jnp.float32), key_rows.astype(jnp.float32)) * scaling
    highest = jnp.max(scores, axis=-1, keepdims=True)
    exponent = jnp.exp(scores - highest)
    denominator = jnp.sum(exponent, axis=-1)
    rounded = lax.optimization_barrier(exponent.astype(jnp.bfloat16))
    numerator = jnp.einsum("rhn,rnd->rhd", rounded.astype(jnp.float32), value_rows.astype(jnp.float32))
    return numerator / denominator[..., None]


def reference(queries, paged_key_cache, paged_value_cache, summary_keys, summary_values, gate_logits, block_group_row, picked):
    group_index = (jnp.arange(SEQUENCE_TOTAL) // SEQ_GRP).astype(jnp.int32)
    block_rows = block_group_row + group_index[:, None] * SLOTS_GRP
    group_arranged = queries.reshape(SEQUENCE_TOTAL * KEY_HEADS, QUERY_PER_KEY, HEAD_SIZE)
    summary_key_rows = summary_keys[:, block_rows].transpose(1, 0, 2, 3).reshape(SEQUENCE_TOTAL * KEY_HEADS, SEQUENCE_BLOCKS, HEAD_SIZE)
    summary_value_rows = summary_values[:, block_rows].transpose(1, 0, 2, 3).reshape(SEQUENCE_TOTAL * KEY_HEADS, SEQUENCE_BLOCKS, HEAD_SIZE)
    compressed = attend(group_arranged, summary_key_rows, summary_value_rows)
    sequence_index = jnp.arange(SEQUENCE_TOTAL).astype(jnp.int32)
    chosen = block_rows[sequence_index[None, :, None], picked]
    head_position = jnp.arange(KEY_HEADS).astype(jnp.int32)[:, None, None]
    picked_keys = paged_key_cache[chosen, head_position]
    picked_values = paged_value_cache[chosen, head_position]
    picked_keys = picked_keys.transpose(1, 0, 2, 3, 4).reshape(SEQUENCE_TOTAL * KEY_HEADS, PICKED_BLOCKS * BLOCK_TOKENS, HEAD_SIZE)
    picked_values = picked_values.transpose(1, 0, 2, 3, 4).reshape(SEQUENCE_TOTAL * KEY_HEADS, PICKED_BLOCKS * BLOCK_TOKENS, HEAD_SIZE)
    selected = attend(group_arranged, picked_keys, picked_values)
    gates = jax.nn.sigmoid(gate_logits)
    attention = gates[0][..., None] * compressed.reshape(SEQUENCE_TOTAL, HQ, HEAD_SIZE) + gates[1][..., None] * selected.reshape(SEQUENCE_TOTAL, HQ, HEAD_SIZE)
    retrieval_counts = jnp.zeros((SEQUENCE_BLOCKS,), jnp.float32).at[picked.reshape(-1)].add(1.0)
    return attention, retrieval_counts
```

```python
import functools

import jax
import jax.numpy as jnp
from jax import lax
from jax.experimental import pallas as pl
from jax.experimental.pallas import tpu as pltpu
from jax.sharding import PartitionSpec as P

VERY_NEGATIVE = -1e30
VMEM = pltpu.VMEM
SMEM = pltpu.SMEM


def fetch_kernel(self_ref, rows_ref, picked_ref, keys_hbm, values_hbm, keys_out, values_out, counts_out, valid_out, key_sem, value_sem, *, slots_here, blocks_each):
    key_heads, sequences, picks = picked_ref.shape
    self_index = self_ref[0]
    block_ids = lax.broadcasted_iota(jnp.int32, counts_out.shape, 1)
    sums = [jnp.zeros(counts_out.shape, jnp.int32) for _ in range(4)]
    for head in range(key_heads):
        for sequence in range(sequences):
            place = jnp.int32(sequence * blocks_each)
            found = jnp.int32(0)
            for pick in range(picks):
                block = picked_ref[head, sequence, pick]
                slot = rows_ref[sequence, block]
                here = slot // slots_here == self_index
                place = jnp.where(here, slot % slots_here, place)
                found = jnp.where(here, 1, found)
                sums[pick % 4] += (block_ids == block).astype(jnp.int32)
            valid_out[head, sequence] = found
            pltpu.make_async_copy(keys_hbm.at[place, head], keys_out.at[head, sequence], key_sem).start()
            pltpu.make_async_copy(values_hbm.at[place, head], values_out.at[head, sequence], value_sem).start()
    counts_out[...] = (sums[0] + sums[1] + (sums[2] + sums[3])).astype(jnp.float32)
    pltpu.make_async_copy(keys_out, keys_out, key_sem).wait()
    pltpu.make_async_copy(values_out, values_out, value_sem).wait()


def fetch(self_index, block_group_row, picked, keys, values):
    key_heads, sequences, _ = picked.shape
    slots_here, _, tokens, width = keys.shape
    blocks = block_group_row.shape[1]
    gathered = jax.ShapeDtypeStruct((key_heads, sequences, tokens, width), keys.dtype)
    nbytes = 2 * key_heads * sequences * tokens * width * 2
    return pl.pallas_call(
        functools.partial(fetch_kernel, slots_here=slots_here, blocks_each=slots_here // sequences),
        out_shape=(
            gathered,
            gathered,
            jax.ShapeDtypeStruct((1, blocks), jnp.float32),
            jax.ShapeDtypeStruct((key_heads, sequences), jnp.int32),
        ),
        in_specs=[
            pl.BlockSpec(memory_space=SMEM),
            pl.BlockSpec(memory_space=SMEM),
            pl.BlockSpec(memory_space=SMEM),
            pl.BlockSpec(memory_space=pl.ANY),
            pl.BlockSpec(memory_space=pl.ANY),
        ],
        out_specs=(
            pl.BlockSpec(memory_space=VMEM),
            pl.BlockSpec(memory_space=VMEM),
            pl.BlockSpec(memory_space=VMEM),
            pl.BlockSpec(memory_space=SMEM),
        ),
        scratch_shapes=[pltpu.SemaphoreType.DMA, pltpu.SemaphoreType.DMA],
        cost_estimate=pl.CostEstimate(flops=0, transcendentals=0, bytes_accessed=2 * nbytes),
        name="fetch",
    )(self_index, block_group_row, picked, keys, values)


def split3(x):
    high = x.astype(jnp.bfloat16).astype(jnp.float32)
    rest = x - high
    middle = rest.astype(jnp.bfloat16).astype(jnp.float32)
    return high, middle, rest - middle


def attend_part(query, keys, values, usable, present):
    scaling = query.shape[-1] ** -0.5
    scores = lax.dot_general(query, keys, (((1,), (1,)), ((), ())), preferred_element_type=jnp.float32) * scaling
    scores = jnp.where(usable, scores, VERY_NEGATIVE)
    highest = jnp.max(scores, axis=-1, keepdims=True)
    exponent = jnp.exp(scores - highest)
    if present is not None:
        exponent = jnp.where(present, exponent, 0.0)
    total = jnp.sum(exponent, axis=-1, keepdims=True)
    numerator = lax.dot_general(
        exponent.astype(jnp.bfloat16), values, (((1,), (0,)), ((), ())), preferred_element_type=jnp.float32
    )
    return highest, total, numerator


def partial_kernel(query_ref, keys_ref, values_ref, summary_keys_ref, summary_values_ref, valid_ref, out_ref, *, heads_here, always):
    key_heads, rows, width = query_ref.shape
    _, sequences, tokens, _ = keys_ref.shape
    slots = summary_keys_ref.shape[1]
    out_rows = out_ref.shape[1] // 3
    per_head = rows // out_rows

    def usable_for(columns, each):
        row = lax.broadcasted_iota(jnp.int32, (rows, columns), 0)
        column = lax.broadcasted_iota(jnp.int32, (rows, columns), 1)
        return (row // heads_here) % sequences == column // each

    usable_block = usable_for(sequences * tokens, tokens)
    usable_summary = usable_for(slots, slots // sequences)
    lane = lax.broadcasted_iota(jnp.int32, (rows, width), 1)
    for head in range(key_heads):
        query = query_ref[head]
        present = None
        usable = usable_block
        if not always:
            column = lax.broadcasted_iota(jnp.int32, (rows, sequences * tokens), 1) // tokens
            flag = jnp.zeros((rows, sequences * tokens), jnp.int32)
            for sequence in range(sequences):
                flag = jnp.where(column == sequence, valid_ref[head, sequence], flag)
            usable = usable_block & (flag > 0)
            present = usable
        keys = keys_ref[head].reshape(sequences * tokens, width)
        values = values_ref[head].reshape(sequences * tokens, width)
        top_s, sum_s, num_s = attend_part(query, keys, values, usable, present)
        top_l, sum_l, num_l = attend_part(query, summary_keys_ref[head], summary_values_ref[head], usable_summary, None)
        stats = jnp.zeros((rows, width), jnp.float32)
        at = 0
        for value in (top_l, sum_l, top_s, sum_s):
            for term in split3(value):
                stats = jnp.where(lane == at, term, stats)
                at += 1
        for part in range(per_head):
            here = slice(part * out_rows, (part + 1) * out_rows)
            target = head * per_head + part
            for i, piece in enumerate((num_l, num_s, stats)):
                out_ref[target, i * out_rows : (i + 1) * out_rows, :] = piece[here].astype(jnp.bfloat16)


def partials(query, keys, values, summary_keys, summary_values, valid, shards, heads_here, always):
    key_heads, rows, width = query.shape
    out_rows = key_heads * rows // shards
    return pl.pallas_call(
        functools.partial(partial_kernel, heads_here=heads_here, always=always),
        out_shape=jax.ShapeDtypeStruct((shards, 3 * out_rows, width), jnp.bfloat16),
        in_specs=[pl.BlockSpec(memory_space=VMEM)] * 5 + [pl.BlockSpec(memory_space=SMEM)],
        out_specs=pl.BlockSpec(memory_space=VMEM),
        name="partials",
    )(query, keys, values, summary_keys, summary_values, valid)


def merge_kernel(parts_ref, gates_ref, out_ref):
    sources, rows3, width = parts_ref.shape
    rows = rows3 // 3
    _, sequences, heads_here = gates_ref.shape
    stats = []
    for source in range(sources):
        raw = parts_ref[source, 2 * rows : 3 * rows, :].astype(jnp.float32)
        stats.append([raw[:, i : i + 1] + raw[:, i + 1 : i + 2] + raw[:, i + 2 : i + 3] for i in (0, 3, 6, 9)])
    row = lax.broadcasted_iota(jnp.int32, (rows, heads_here), 0)
    column = lax.broadcasted_iota(jnp.int32, (rows, heads_here), 1)
    result = None
    for branch in range(2):
        highest = functools.reduce(jnp.maximum, [s[2 * branch] for s in stats])
        total = jnp.zeros((rows, 1), jnp.float32)
        numerator = jnp.zeros((rows, width), jnp.float32)
        for source in range(sources):
            weight = jnp.exp(stats[source][2 * branch] - highest)
            total += weight * stats[source][2 * branch + 1]
            numerator += weight * parts_ref[source, branch * rows : (branch + 1) * rows, :].astype(jnp.float32)
        gate = 1.0 / (1.0 + jnp.exp(-gates_ref[branch]))
        spread = jnp.zeros((rows, heads_here), jnp.float32)
        for sequence in range(sequences):
            spread = jnp.where(row // heads_here == sequence, gate[sequence : sequence + 1, :], spread)
        spread = jnp.sum(jnp.where(column == row % heads_here, spread, 0.0), axis=1, keepdims=True)
        term = numerator * (spread / total)
        result = term if result is None else result + term
    out_ref[...] = result


def merge(parts, gates):
    rows = parts.shape[1] // 3
    return pl.pallas_call(
        merge_kernel,
        out_shape=jax.ShapeDtypeStruct((rows, parts.shape[2]), jnp.float32),
        in_specs=[pl.BlockSpec(memory_space=VMEM)] * 2,
        out_specs=pl.BlockSpec(memory_space=VMEM),
        name="merge",
    )(parts, gates)


def sum_over(value, axis):
    size = lax.axis_size(axis)
    if size & (size - 1):
        total = value
        for step in range(1, size):
            total = total + lax.ppermute(value, axis, [(i, (i + step) % size) for i in range(size)])
        return total
    step = 1
    while step < size:
        value = value + lax.ppermute(value, axis, [(i, i ^ step) for i in range(size)])
        step *= 2
    return value


def body(
    queries,
    paged_key_cache,
    paged_value_cache,
    summary_keys,
    summary_values,
    gate_logits,
    block_group_row,
    picked,
):
    shards = lax.axis_size("shard")
    self_index = lax.axis_index("shard").astype(jnp.int32).reshape(1)
    sequences, heads_here, width = queries.shape
    key_heads, _, picks = picked.shape
    rows = sequences * heads_here
    copies = jnp.broadcast_to(queries.reshape(1, rows, width), (shards, rows, width))
    everyone = lax.all_to_all(copies, "shard", split_axis=0, concat_axis=0, tiled=True)
    everyone = everyone.reshape(key_heads, shards * rows // key_heads, width)
    keys, values, counts, valid = fetch(self_index, block_group_row, picked, paged_key_cache, paged_value_cache)
    outgoing = partials(
        everyone, keys, values, summary_keys, summary_values, valid, shards, heads_here, shards == picks
    )
    incoming = lax.all_to_all(outgoing, "shard", split_axis=0, concat_axis=0, tiled=True)
    attention = merge(incoming, gate_logits).reshape(sequences, heads_here, width)
    retrieval_counts = sum_over(counts, "grp").reshape(-1)
    return attention, retrieval_counts


def solution(mesh):
    placed = (
        P("grp", "shard", None),
        P(("grp", "shard"), None, None, None),
        P(("grp", "shard"), None, None, None),
        P(None, ("grp", "shard"), None),
        P(None, ("grp", "shard"), None),
        P(None, "grp", "shard"),
        P("grp", None),
        P(None, "grp", None),
    )
    return jax.shard_map(
        body, mesh=mesh, in_specs=placed, out_specs=(P("grp", "shard", None), P()), check_vma=False
    )
```

```python
import functools

import jax
import jax.numpy as jnp
from jax import lax
from jax.experimental import pallas as pl
from jax.experimental.pallas import tpu as pltpu
from jax.sharding import PartitionSpec as P


VERY_NEGATIVE = -1e30
VMEM = pltpu.VMEM
SMEM = pltpu.SMEM
LIMIT = 4 * 1024 * 1024


def fetch_kernel(rows_hbm, picked_hbm, keys_hbm, values_hbm, keys_out, values_out, counts_out, *refs, slots_here, blocks_each):
    valid_out = refs[0] if len(refs) == 9 else None
    rows_ref, picked_ref, picked_tile, rows_sem, picked_sem, tile_sem, key_sem, value_sem = refs[-8:]
    copies = [
        pltpu.make_async_copy(rows_hbm, rows_ref, rows_sem),
        pltpu.make_async_copy(picked_hbm, picked_ref, picked_sem),
        pltpu.make_async_copy(picked_hbm, picked_tile, tile_sem),
    ]
    for copy in copies:
        copy.start()
    key_heads, sequences, picks = picked_ref.shape
    first = lax.axis_index("shard") * slots_here
    for copy in copies[:2]:
        copy.wait()
    for head in range(key_heads):
        for sequence in range(sequences):
            place = jnp.int32(sequence * blocks_each)
            found = jnp.int32(0)
            for pick in range(picks):
                slot = rows_ref[sequence, picked_ref[head, sequence, pick]] - first
                here = (slot >= 0) & (slot < slots_here)
                place = jnp.where(here, slot, place)
                found = jnp.where(here, 1, found)
            if valid_out is not None:
                valid_out[head, sequence] = found
            pltpu.make_async_copy(keys_hbm.at[place, head], keys_out.at[head, sequence], key_sem).start()
            pltpu.make_async_copy(values_hbm.at[place, head], values_out.at[head, sequence], value_sem).start()
    copies[2].wait()
    told_rows, width = counts_out.shape
    counts = []
    for row in range(told_rows):
        sums = [jnp.zeros((sequences, width), jnp.float32) for _ in range(2)]
        if row * width < rows_ref.shape[1]:
            block_ids = lax.broadcasted_iota(jnp.int32, (sequences, width), 1) + row * width
            for head in range(key_heads):
                tile = picked_tile[head]
                for pick in range(picks):
                    sums[pick % 2] += jnp.where(tile[:, pick : pick + 1] == block_ids, 1.0, 0.0)
        counts.append(jnp.sum(sums[0] + sums[1], axis=0, keepdims=True))
    counts_out[...] = jnp.concatenate(counts, axis=0).astype(jnp.bfloat16)
    pltpu.make_async_copy(keys_out, keys_out, key_sem).wait()
    pltpu.make_async_copy(values_out, values_out, value_sem).wait()


def fetch(block_group_row, picked, keys, values, always):
    key_heads, sequences, _ = picked.shape
    slots_here, _, tokens, width = keys.shape
    gathered = jax.ShapeDtypeStruct((key_heads, sequences, tokens, width), keys.dtype)
    told_rows = -(-block_group_row.shape[1] // (8 * width)) * 8
    nbytes = 2 * key_heads * sequences * tokens * width * 2
    out_shape = [gathered, gathered, jax.ShapeDtypeStruct((told_rows, width), jnp.bfloat16)]
    out_specs = [pl.BlockSpec(memory_space=VMEM)] * 3
    if not always:
        out_shape.append(jax.ShapeDtypeStruct((key_heads, sequences), jnp.int32))
        out_specs.append(pl.BlockSpec(memory_space=SMEM))
    out = pl.pallas_call(
        functools.partial(fetch_kernel, slots_here=slots_here, blocks_each=slots_here // sequences),
        out_shape=out_shape,
        in_specs=[pl.BlockSpec(memory_space=pltpu.HBM)] * 4,
        out_specs=out_specs,
        scratch_shapes=[
            SMEM(block_group_row.shape, jnp.int32),
            SMEM(picked.shape, jnp.int32),
            VMEM(picked.shape, jnp.int32),
        ]
        + [pltpu.SemaphoreType.DMA] * 5,
        cost_estimate=pl.CostEstimate(flops=0, transcendentals=0, bytes_accessed=2 * nbytes),
        compiler_params=pltpu.CompilerParams(vmem_limit_bytes=LIMIT),
        name="fetch",
    )(*(pltpu.with_memory_space_constraint(x, pltpu.HBM) for x in (block_group_row, picked, keys, values)))
    return out[0], out[1], out[2], None if always else out[3]


def split3(x):
    high = x.astype(jnp.bfloat16).astype(jnp.float32)
    rest = x - high
    middle = rest.astype(jnp.bfloat16).astype(jnp.float32)
    return high, middle, rest - middle


def attend_part(query, keys, values, usable, present):
    scaling = query.shape[-1] ** -0.5
    scores = lax.dot_general(query, keys, (((1,), (1,)), ((), ())), preferred_element_type=jnp.float32) * scaling
    scores = jnp.where(usable, scores, VERY_NEGATIVE)
    highest = jnp.max(scores, axis=-1, keepdims=True)
    exponent = jnp.exp(scores - highest)
    if present is not None:
        exponent = jnp.where(present, exponent, 0.0)
    total = jnp.sum(exponent, axis=-1, keepdims=True)
    numerator = lax.dot_general(
        exponent.astype(jnp.bfloat16), values, (((1,), (0,)), ((), ())), preferred_element_type=jnp.float32
    )
    return highest, total, numerator


def usable_for(rows, columns, each, heads_here, sequences):
    row = lax.broadcasted_iota(jnp.int32, (rows, columns), 0)
    column = lax.broadcasted_iota(jnp.int32, (rows, columns), 1)
    return (row // heads_here) % sequences == column // each


def partial_kernel(query_ref, keys_ref, values_ref, summary_keys_ref, summary_values_ref, told_ref, *refs, heads_here):
    valid_ref = refs[0] if len(refs) == 2 else None
    out_ref = refs[-1]
    key_heads, rows, width = query_ref.shape
    _, sequences, tokens, _ = keys_ref.shape
    slots = summary_keys_ref.shape[1]
    shards, sent_rows, _ = out_ref.shape
    told_rows = told_ref.shape[0]
    out_rows = (sent_rows - told_rows) // 3
    per_head = rows // out_rows

    usable_block = usable_for(rows, sequences * tokens, tokens, heads_here, sequences)
    usable_summary = usable_for(rows, slots, slots // sequences, heads_here, sequences)
    lane = lax.broadcasted_iota(jnp.int32, (rows, width), 1)
    for shard in range(shards):
        out_ref[shard, 3 * out_rows :, :] = told_ref[...]
    for head in range(key_heads):
        query = query_ref[head]
        present = None
        usable = usable_block
        if valid_ref is not None:
            column = lax.broadcasted_iota(jnp.int32, (rows, sequences * tokens), 1) // tokens
            flag = jnp.zeros((rows, sequences * tokens), jnp.int32)
            for sequence in range(sequences):
                flag = jnp.where(column == sequence, valid_ref[head, sequence], flag)
            usable = usable_block & (flag > 0)
            present = usable
        keys = keys_ref[head].reshape(sequences * tokens, width)
        values = values_ref[head].reshape(sequences * tokens, width)
        top_s, sum_s, num_s = attend_part(query, keys, values, usable, present)
        top_l, sum_l, num_l = attend_part(query, summary_keys_ref[head], summary_values_ref[head], usable_summary, None)
        stats = jnp.zeros((rows, width), jnp.float32)
        at = 0
        for value in (top_l, sum_l, top_s, sum_s):
            for term in split3(value):
                stats = jnp.where(lane == at, term, stats)
                at += 1
        for part in range(per_head):
            here = slice(part * out_rows, (part + 1) * out_rows)
            target = head * per_head + part
            for i, piece in enumerate((num_l, num_s, stats)):
                out_ref[target, i * out_rows : (i + 1) * out_rows, :] = piece[here].astype(jnp.bfloat16)


def partials(query, keys, values, summary_keys, summary_values, told, valid, shards, heads_here):
    key_heads, rows, width = query.shape
    out_rows = key_heads * rows // shards
    operands = [query, keys, values, summary_keys, summary_values, told]
    in_specs = [pl.BlockSpec(memory_space=VMEM)] * 6
    if valid is not None:
        operands.append(valid)
        in_specs.append(pl.BlockSpec(memory_space=SMEM))
    return pl.pallas_call(
        functools.partial(partial_kernel, heads_here=heads_here),
        out_shape=jax.ShapeDtypeStruct((shards, 3 * out_rows + told.shape[0], width), jnp.bfloat16),
        in_specs=in_specs,
        out_specs=pl.BlockSpec(memory_space=VMEM),
        compiler_params=pltpu.CompilerParams(vmem_limit_bytes=LIMIT),
        name="partials",
    )(*operands)


def merge_kernel(parts_ref, gates_ref, counts_ref, out_ref, counts_out, *, tellers):
    sources, sent_rows, width = parts_ref.shape
    told_rows = counts_ref.shape[0]
    rows = (sent_rows - told_rows) // 3
    _, sequences, heads_here = gates_ref.shape
    counts = counts_ref[...].astype(jnp.float32)
    for teller in range(tellers):
        counts += parts_ref[teller, 3 * rows :, :].astype(jnp.float32)
    counts_out[...] = counts[: counts_out.shape[0]]
    stats = []
    for source in range(sources):
        raw = parts_ref[source, 2 * rows : 3 * rows, :].astype(jnp.float32)
        stats.append([raw[:, i : i + 1] + raw[:, i + 1 : i + 2] + raw[:, i + 2 : i + 3] for i in (0, 3, 6, 9)])
    row = lax.broadcasted_iota(jnp.int32, (rows, heads_here), 0)
    column = lax.broadcasted_iota(jnp.int32, (rows, heads_here), 1)
    result = None
    for branch in range(2):
        highest = functools.reduce(jnp.maximum, [s[2 * branch] for s in stats])
        total = jnp.zeros((rows, 1), jnp.float32)
        numerator = jnp.zeros((rows, width), jnp.float32)
        for source in range(sources):
            weight = jnp.exp(stats[source][2 * branch] - highest)
            total += weight * stats[source][2 * branch + 1]
            numerator += weight * parts_ref[source, branch * rows : (branch + 1) * rows, :].astype(jnp.float32)
        gate = 1.0 / (1.0 + jnp.exp(-gates_ref[branch]))
        spread = jnp.zeros((rows, heads_here), jnp.float32)
        for sequence in range(sequences):
            spread = jnp.where(row // heads_here == sequence, gate[sequence : sequence + 1, :], spread)
        spread = jnp.sum(jnp.where(column == row % heads_here, spread, 0.0), axis=1, keepdims=True)
        term = numerator * (spread / total)
        result = term if result is None else result + term
    out_ref[...] = result


def merge(parts, gates, counts, count_rows, tellers):
    rows = (parts.shape[1] - counts.shape[0]) // 3
    width = parts.shape[2]
    return pl.pallas_call(
        functools.partial(merge_kernel, tellers=tellers),
        out_shape=(
            jax.ShapeDtypeStruct((rows, width), jnp.float32),
            jax.ShapeDtypeStruct((count_rows, width), jnp.float32),
        ),
        in_specs=[pl.BlockSpec(memory_space=VMEM)] * 3,
        out_specs=(pl.BlockSpec(memory_space=VMEM),) * 2,
        compiler_params=pltpu.CompilerParams(vmem_limit_bytes=LIMIT),
        name="merge",
    )(parts, gates, counts)


def half_kernel(query_ref, keys_ref, values_ref, summary_keys_ref, summary_values_ref, out_ref, *, heads_here, flip):
    chips, rows, width = query_ref.shape
    _, sequences, tokens, _ = keys_ref.shape
    slots = summary_keys_ref.shape[1]
    me = lax.axis_index("shard")
    chip, core = me // 2, me % 2
    if flip:
        core = 1 - core
    usable_block = usable_for(rows, sequences * tokens, tokens, heads_here, sequences)
    usable_summary = usable_for(rows, slots, slots // sequences, heads_here, sequences)
    lane = lax.broadcasted_iota(jnp.int32, (rows, width), 1)
    for step in range(chips):
        head = lax.rem(chip + (chips - step), chips) * 2 + core
        query = query_ref[step]
        keys = keys_ref[head].reshape(sequences * tokens, width)
        values = values_ref[head].reshape(sequences * tokens, width)
        top_s, sum_s, num_s = attend_part(query, keys, values, usable_block, None)
        top_l, sum_l, num_l = attend_part(query, summary_keys_ref[head], summary_values_ref[head], usable_summary, None)
        stats = jnp.where(lane == 0, top_l, jnp.where(lane == 1, sum_l, jnp.where(lane == 2, top_s, sum_s)))
        out_ref[step, :rows, :] = num_l
        out_ref[step, rows : 2 * rows, :] = num_s
        out_ref[step, 2 * rows :, :] = stats


def half(query, keys, values, summary_keys, summary_values, heads_here, flip):
    chips, rows, width = query.shape
    return pl.pallas_call(
        functools.partial(half_kernel, heads_here=heads_here, flip=flip),
        out_shape=jax.ShapeDtypeStruct((chips, 3 * rows, width), jnp.float32),
        in_specs=[pl.BlockSpec(memory_space=VMEM)] * 5,
        out_specs=pl.BlockSpec(memory_space=VMEM),
        cost_estimate=pl.CostEstimate(flops=10**8, transcendentals=10**5, bytes_accessed=10**6),
        compiler_params=pltpu.CompilerParams(vmem_limit_bytes=LIMIT),
        name="other_half" if flip else "own_half",
    )(query, keys, values, summary_keys, summary_values)


def join_kernel(own_ref, other_ref, told_ref, *out_refs, silent):
    chips, rows3, width = own_ref.shape
    told = jnp.where(lax.axis_index("shard") // 2 == silent, 0.0, told_ref[...].astype(jnp.float32)).astype(jnp.bfloat16)
    rows = rows3 // 3
    lane = lax.broadcasted_iota(jnp.int32, (rows, width), 1)
    for step in range(chips):
        out_ref = out_refs[step]
        own_stats = own_ref[step, 2 * rows :, :]
        other_stats = other_ref[step, 2 * rows :, :]
        stats = jnp.zeros((rows, width), jnp.float32)
        at = 0
        for branch in range(2):
            here = slice(branch * rows, (branch + 1) * rows)
            own_top, other_top = own_stats[:, 2 * branch : 2 * branch + 1], other_stats[:, 2 * branch : 2 * branch + 1]
            own_sum, other_sum = own_stats[:, 2 * branch + 1 : 2 * branch + 2], other_stats[:, 2 * branch + 1 : 2 * branch + 2]
            highest = jnp.maximum(own_top, other_top)
            own_weight, other_weight = jnp.exp(own_top - highest), jnp.exp(other_top - highest)
            numerator = own_weight * own_ref[step, here, :] + other_weight * other_ref[step, here, :]
            out_ref[here, :] = numerator.astype(jnp.bfloat16)
            for value in (highest, own_weight * own_sum + other_weight * other_sum):
                for term in split3(value):
                    stats = jnp.where(lane == at, term, stats)
                    at += 1
        out_ref[2 * rows : 3 * rows, :] = stats.astype(jnp.bfloat16)
        out_ref[3 * rows :, :] = told


def join(own, other, told, silent):
    chips, rows3, width = own.shape
    shape = jax.ShapeDtypeStruct((rows3 + told.shape[0], width), jnp.bfloat16)
    return pl.pallas_call(
        functools.partial(join_kernel, silent=silent),
        out_shape=[shape] * chips,
        in_specs=[pl.BlockSpec(memory_space=VMEM)] * 3,
        out_specs=[pl.BlockSpec(memory_space=VMEM)] * chips,
        compiler_params=pltpu.CompilerParams(vmem_limit_bytes=LIMIT),
        name="join",
    )(own, other, told)


def finish_kernel(*refs):
    *part_refs, gates_ref, counts_ref, out_ref, counts_out = refs
    rows, width = out_ref.shape
    _, sequences, heads_here = gates_ref.shape
    counts = counts_ref[...].astype(jnp.float32) + sum(ref[3 * rows :, :].astype(jnp.float32) for ref in part_refs)
    counts_out[...] = counts[: counts_out.shape[0]]
    row = lax.broadcasted_iota(jnp.int32, (rows, heads_here), 0)
    column = lax.broadcasted_iota(jnp.int32, (rows, heads_here), 1)
    stats = []
    for ref in part_refs:
        raw = ref[2 * rows : 3 * rows, :].astype(jnp.float32)
        stats.append([raw[:, i : i + 1] + raw[:, i + 1 : i + 2] + raw[:, i + 2 : i + 3] for i in (0, 3, 6, 9)])
    result = jnp.zeros((rows, width), jnp.float32)
    for branch in range(2):
        highest = functools.reduce(jnp.maximum, [s[2 * branch] for s in stats])
        weights = [jnp.exp(s[2 * branch] - highest) for s in stats]
        total = sum(weight * s[2 * branch + 1] for weight, s in zip(weights, stats))
        here = slice(branch * rows, (branch + 1) * rows)
        numerator = sum(weight * ref[here, :].astype(jnp.float32) for weight, ref in zip(weights, part_refs))
        gate = 1.0 / (1.0 + jnp.exp(-gates_ref[branch]))
        spread = jnp.zeros((rows, heads_here), jnp.float32)
        for sequence in range(sequences):
            spread = jnp.where(row // heads_here == sequence, gate[sequence : sequence + 1, :], spread)
        spread = jnp.sum(jnp.where(column == row % heads_here, spread, 0.0), axis=1, keepdims=True)
        result += numerator * (spread / total)
    out_ref[...] = result


def finish(parts, gates, counts, rows, count_rows):
    width = parts[0].shape[1]
    return pl.pallas_call(
        finish_kernel,
        out_shape=(
            jax.ShapeDtypeStruct((rows, width), jnp.float32),
            jax.ShapeDtypeStruct((count_rows, width), jnp.float32),
        ),
        in_specs=[pl.BlockSpec(memory_space=VMEM)] * (len(parts) + 2),
        out_specs=(pl.BlockSpec(memory_space=VMEM),) * 2,
        compiler_params=pltpu.CompilerParams(vmem_limit_bytes=LIMIT),
        name="finish",
    )(*parts, gates, counts)


def by_chips(queries, keys_cache, values_cache, summary_keys, summary_values, gate_logits, block_group_row, picked):
    groups, shards = lax.axis_size("grp"), lax.axis_size("shard")
    chips = shards // 2
    sequences, heads_here, width = queries.shape
    blocks = block_group_row.shape[1]
    rows = sequences * heads_here

    def shift(step):
        return [(s, (s // 2 + step) % chips * 2 + s % 2) for s in range(shards)]

    partner = [(s, s ^ 1) for s in range(shards)]
    mine = queries.reshape(rows, width)
    arrived = []
    for step in range(1, chips):
        arrived.append(lax.ppermute(mine, "shard", shift(step)))
    keys, values, counts, _ = fetch(block_group_row, picked, keys_cache, values_cache, True)
    offsets = [groups - 1 if chip == groups - 1 else chip % (groups - 2) + 1 for chip in range(chips)] if groups > 2 else [1] * chips
    pairs = [
        ((group ^ offsets[shard // 2]) * shards + shard, group * shards + shard)
        for group in range(groups)
        for shard in range(shards)
    ]
    told = lax.ppermute(counts, ("grp", "shard"), pairs)
    own_query = jnp.stack([mine] + arrived)
    other_query = lax.ppermute(own_query, "shard", partner)
    own = half(own_query, keys, values, summary_keys, summary_values, heads_here, False)
    other = half(other_query, keys, values, summary_keys, summary_values, heads_here, True)
    other = lax.ppermute(other, "shard", partner)
    parts = list(join(own, other, told, groups - 2))
    for step in range(1, chips):
        parts[step] = lax.ppermute(parts[step], "shard", shift(-step))
    attention, retrieval_counts = finish(parts, gate_logits, counts, rows, blocks // width)
    return attention.reshape(sequences, heads_here, width), retrieval_counts.reshape(-1)


def body(
    queries,
    paged_key_cache,
    paged_value_cache,
    summary_keys,
    summary_values,
    gate_logits,
    block_group_row,
    picked,
):
    groups, shards = lax.axis_size("grp"), lax.axis_size("shard")
    sequences, heads_here, width = queries.shape
    key_heads, _, picks = picked.shape
    blocks = block_group_row.shape[1]
    rows = sequences * heads_here
    always = shards == picks
    if shards == key_heads == picks and shards == 2 * groups and groups & (groups - 1) == 0:
        return by_chips(
            queries, paged_key_cache, paged_value_cache, summary_keys, summary_values, gate_logits, block_group_row, picked
        )

    keys, values, counts, valid = fetch(block_group_row, picked, paged_key_cache, paged_value_cache, always)
    tellers = groups - 1
    pairs = [
        ((group + 1 + shard) % groups * shards + shard, group * shards + shard)
        for group in range(groups)
        for shard in range(tellers)
    ]
    told = lax.ppermute(counts, ("grp", "shard"), pairs)

    copies = jnp.broadcast_to(queries.reshape(1, rows, width), (shards, rows, width))
    everyone = lax.all_to_all(copies, "shard", split_axis=0, concat_axis=0, tiled=True)
    everyone = everyone.reshape(key_heads, shards * rows // key_heads, width)
    outgoing = partials(everyone, keys, values, summary_keys, summary_values, told, valid, shards, heads_here)
    incoming = lax.all_to_all(outgoing, "shard", split_axis=0, concat_axis=0, tiled=True)
    attention, retrieval_counts = merge(incoming, gate_logits, counts, blocks // width, tellers)
    return attention.reshape(sequences, heads_here, width), retrieval_counts.reshape(-1)


def solution(mesh):
    placed = (
        P("grp", "shard", None),
        P(("grp", "shard"), None, None, None),
        P(("grp", "shard"), None, None, None),
        P(None, ("grp", "shard"), None),
        P(None, ("grp", "shard"), None),
        P(None, "grp", "shard"),
        P("grp", None),
        P(None, "grp", None),
    )
    return jax.shard_map(
        body, mesh=mesh, in_specs=placed, out_specs=(P("grp", "shard", None), P()), check_vma=False
    )
```

```python
import functools

import jax
import jax.numpy as jnp
from jax import lax
from jax.experimental import pallas as pl
from jax.experimental.pallas import tpu as pltpu
from jax.sharding import PartitionSpec as P


VERY_NEGATIVE = -1e30
VMEM = pltpu.VMEM
SMEM = pltpu.SMEM
LIMIT = 4 * 1024 * 1024


def fetch_kernel(rows_hbm, picked_hbm, keys_hbm, values_hbm, keys_out, values_out, counts_out, *refs, slots_here, blocks_each, with_valid):
    valid_out = refs[0] if with_valid else None
    sequences, blocks = rows_hbm.shape
    *rows_refs, picked_ref, picked_tile, rows_sem, picked_sem, tile_sem, key_sem, value_sem = refs[-7 - sequences :]
    copies = [pltpu.make_async_copy(rows_hbm.at[i], ref, rows_sem.at[i]) for i, ref in enumerate(rows_refs)]
    copies.append(pltpu.make_async_copy(picked_hbm, picked_ref, picked_sem))
    copies.append(pltpu.make_async_copy(picked_hbm, picked_tile, tile_sem))
    for copy in copies:
        copy.start()
    key_heads, _, picks = picked_ref.shape
    first = lax.axis_index("shard") * slots_here
    for copy in copies[:-1]:
        copy.wait()
    for head in range(key_heads):
        for sequence in range(sequences):
            places = []
            for pick in range(picks):
                slot = rows_refs[sequence][picked_ref[head, sequence, pick]]
                if slots_here & (slots_here - 1) == 0:
                    places.append(slot ^ first)
                else:
                    places.append(jnp.where(slot >= first, slot - first, slots_here))
            while len(places) > 1:
                places = [functools.reduce(jnp.minimum, places[i : i + 2]) for i in range(0, len(places), 2)]
            place = places[0]
            if valid_out is not None:
                found = place < slots_here
                valid_out[head, sequence] = found.astype(jnp.int32)
                place = jnp.where(found, place, sequence * blocks_each)
            pltpu.make_async_copy(keys_hbm.at[place, head], keys_out.at[head, sequence], key_sem).start()
            pltpu.make_async_copy(values_hbm.at[place, head], values_out.at[head, sequence], value_sem).start()
    copies[-1].wait()
    told_rows, width = counts_out.shape
    counts = []
    for row in range(told_rows):
        sums = [jnp.zeros((sequences, width), jnp.float32) for _ in range(2)]
        if row * width < blocks:
            block_ids = lax.broadcasted_iota(jnp.int32, (sequences, width), 1) + row * width
            for head in range(key_heads):
                tile = picked_tile[head]
                for pick in range(picks):
                    sums[pick % 2] += jnp.where(tile[:, pick : pick + 1] == block_ids, 1.0, 0.0)
        counts.append(jnp.sum(sums[0] + sums[1], axis=0, keepdims=True))
    counts_out[...] = jnp.concatenate(counts, axis=0).astype(jnp.bfloat16)
    pltpu.make_async_copy(keys_out, keys_out, key_sem).wait()
    pltpu.make_async_copy(values_out, values_out, value_sem).wait()


def fetch(block_group_row, picked, keys, values, always):
    key_heads, sequences, _ = picked.shape
    slots_here, _, tokens, width = keys.shape
    gathered = jax.ShapeDtypeStruct((key_heads, sequences, tokens, width), keys.dtype)
    told_rows = -(-block_group_row.shape[1] // (8 * width)) * 8
    nbytes = 2 * key_heads * sequences * tokens * width * 2
    out_shape = [gathered, gathered, jax.ShapeDtypeStruct((told_rows, width), jnp.bfloat16)]
    out_specs = [pl.BlockSpec(memory_space=VMEM)] * 3
    if not always:
        out_shape.append(jax.ShapeDtypeStruct((key_heads, sequences), jnp.int32))
        out_specs.append(pl.BlockSpec(memory_space=SMEM))
    out = pl.pallas_call(
        functools.partial(
            fetch_kernel, slots_here=slots_here, blocks_each=slots_here // sequences, with_valid=not always
        ),
        out_shape=out_shape,
        in_specs=[pl.BlockSpec(memory_space=pltpu.HBM)] * 4,
        out_specs=out_specs,
        scratch_shapes=[SMEM(block_group_row.shape[1:], jnp.int32)] * sequences
        + [SMEM(picked.shape, jnp.int32), VMEM(picked.shape, jnp.int32), pltpu.SemaphoreType.DMA((sequences,))]
        + [pltpu.SemaphoreType.DMA] * 4,
        cost_estimate=pl.CostEstimate(flops=0, transcendentals=0, bytes_accessed=2 * nbytes),
        compiler_params=pltpu.CompilerParams(vmem_limit_bytes=LIMIT),
        name="fetch",
    )(*(pltpu.with_memory_space_constraint(x, pltpu.HBM) for x in (block_group_row, picked, keys, values)))
    return out[0], out[1], out[2], None if always else out[3]


def split3(x):
    high = x.astype(jnp.bfloat16).astype(jnp.float32)
    rest = x - high
    middle = rest.astype(jnp.bfloat16).astype(jnp.float32)
    return high, middle, rest - middle


def attend_part(query, keys, values, usable, present):
    scaling = query.shape[-1] ** -0.5
    scores = lax.dot_general(query, keys, (((1,), (1,)), ((), ())), preferred_element_type=jnp.float32) * scaling
    scores = jnp.where(usable, scores, VERY_NEGATIVE)
    highest = jnp.max(scores, axis=-1, keepdims=True)
    exponent = jnp.exp(scores - highest)
    if present is not None:
        exponent = jnp.where(present, exponent, 0.0)
    total = jnp.sum(exponent, axis=-1, keepdims=True)
    numerator = lax.dot_general(
        exponent.astype(jnp.bfloat16), values, (((1,), (0,)), ((), ())), preferred_element_type=jnp.float32
    )
    return highest, total, numerator


def usable_for(rows, columns, each, heads_here, sequences):
    row = lax.broadcasted_iota(jnp.int32, (rows, columns), 0)
    column = lax.broadcasted_iota(jnp.int32, (rows, columns), 1)
    return (row // heads_here) % sequences == column // each


def partial_kernel(query_ref, keys_ref, values_ref, summary_keys_ref, summary_values_ref, told_ref, *refs, heads_here):
    valid_ref = refs[0] if len(refs) == 2 else None
    out_ref = refs[-1]
    key_heads, rows, width = query_ref.shape
    _, sequences, tokens, _ = keys_ref.shape
    slots = summary_keys_ref.shape[1]
    shards, sent_rows, _ = out_ref.shape
    told_rows = told_ref.shape[0]
    out_rows = (sent_rows - told_rows) // 3
    per_head = rows // out_rows

    usable_block = usable_for(rows, sequences * tokens, tokens, heads_here, sequences)
    usable_summary = usable_for(rows, slots, slots // sequences, heads_here, sequences)
    lane = lax.broadcasted_iota(jnp.int32, (rows, width), 1)
    for shard in range(shards):
        out_ref[shard, 3 * out_rows :, :] = told_ref[...]
    for head in range(key_heads):
        query = query_ref[head]
        present = None
        usable = usable_block
        if valid_ref is not None:
            column = lax.broadcasted_iota(jnp.int32, (rows, sequences * tokens), 1) // tokens
            flag = jnp.zeros((rows, sequences * tokens), jnp.int32)
            for sequence in range(sequences):
                flag = jnp.where(column == sequence, valid_ref[head, sequence], flag)
            usable = usable_block & (flag > 0)
            present = usable
        keys = keys_ref[head].reshape(sequences * tokens, width)
        values = values_ref[head].reshape(sequences * tokens, width)
        top_s, sum_s, num_s = attend_part(query, keys, values, usable, present)
        top_l, sum_l, num_l = attend_part(query, summary_keys_ref[head], summary_values_ref[head], usable_summary, None)
        stats = jnp.zeros((rows, width), jnp.float32)
        at = 0
        for value in (top_l, sum_l, top_s, sum_s):
            for term in split3(value):
                stats = jnp.where(lane == at, term, stats)
                at += 1
        for part in range(per_head):
            here = slice(part * out_rows, (part + 1) * out_rows)
            target = head * per_head + part
            for i, piece in enumerate((num_l, num_s, stats)):
                out_ref[target, i * out_rows : (i + 1) * out_rows, :] = piece[here].astype(jnp.bfloat16)


def partials(query, keys, values, summary_keys, summary_values, told, valid, shards, heads_here):
    key_heads, rows, width = query.shape
    out_rows = key_heads * rows // shards
    operands = [query, keys, values, summary_keys, summary_values, told]
    in_specs = [pl.BlockSpec(memory_space=VMEM)] * 6
    if valid is not None:
        operands.append(valid)
        in_specs.append(pl.BlockSpec(memory_space=SMEM))
    return pl.pallas_call(
        functools.partial(partial_kernel, heads_here=heads_here),
        out_shape=jax.ShapeDtypeStruct((shards, 3 * out_rows + told.shape[0], width), jnp.bfloat16),
        in_specs=in_specs,
        out_specs=pl.BlockSpec(memory_space=VMEM),
        compiler_params=pltpu.CompilerParams(vmem_limit_bytes=LIMIT),
        name="partials",
    )(*operands)


def merge_kernel(parts_ref, gates_ref, counts_ref, out_ref, counts_out, *, tellers):
    sources, sent_rows, width = parts_ref.shape
    told_rows = counts_ref.shape[0]
    rows = (sent_rows - told_rows) // 3
    _, sequences, heads_here = gates_ref.shape
    counts = counts_ref[...].astype(jnp.float32)
    for teller in range(tellers):
        counts += parts_ref[teller, 3 * rows :, :].astype(jnp.float32)
    counts_out[...] = counts[: counts_out.shape[0]]
    stats = []
    for source in range(sources):
        raw = parts_ref[source, 2 * rows : 3 * rows, :].astype(jnp.float32)
        stats.append([raw[:, i : i + 1] + raw[:, i + 1 : i + 2] + raw[:, i + 2 : i + 3] for i in (0, 3, 6, 9)])
    row = lax.broadcasted_iota(jnp.int32, (rows, heads_here), 0)
    column = lax.broadcasted_iota(jnp.int32, (rows, heads_here), 1)
    result = None
    for branch in range(2):
        highest = functools.reduce(jnp.maximum, [s[2 * branch] for s in stats])
        total = jnp.zeros((rows, 1), jnp.float32)
        numerator = jnp.zeros((rows, width), jnp.float32)
        for source in range(sources):
            weight = jnp.exp(stats[source][2 * branch] - highest)
            total += weight * stats[source][2 * branch + 1]
            numerator += weight * parts_ref[source, branch * rows : (branch + 1) * rows, :].astype(jnp.float32)
        gate = 1.0 / (1.0 + jnp.exp(-gates_ref[branch]))
        spread = jnp.zeros((rows, heads_here), jnp.float32)
        for sequence in range(sequences):
            spread = jnp.where(row // heads_here == sequence, gate[sequence : sequence + 1, :], spread)
        spread = jnp.sum(jnp.where(column == row % heads_here, spread, 0.0), axis=1, keepdims=True)
        term = numerator * (spread / total)
        result = term if result is None else result + term
    out_ref[...] = result


def merge(parts, gates, counts, count_rows, tellers):
    rows = (parts.shape[1] - counts.shape[0]) // 3
    width = parts.shape[2]
    return pl.pallas_call(
        functools.partial(merge_kernel, tellers=tellers),
        out_shape=(
            jax.ShapeDtypeStruct((rows, width), jnp.float32),
            jax.ShapeDtypeStruct((count_rows, width), jnp.float32),
        ),
        in_specs=[pl.BlockSpec(memory_space=VMEM)] * 3,
        out_specs=(pl.BlockSpec(memory_space=VMEM),) * 2,
        compiler_params=pltpu.CompilerParams(vmem_limit_bytes=LIMIT),
        name="merge",
    )(parts, gates, counts)


def half_kernel(query_ref, keys_ref, values_ref, summary_keys_ref, summary_values_ref, out_ref, *, heads_here, flip):
    chips, rows, width = query_ref.shape
    _, sequences, tokens, _ = keys_ref.shape
    slots = summary_keys_ref.shape[1]
    scaling = width**-0.5
    me = lax.axis_index("shard")
    chip, core = me // 2, me % 2
    if flip:
        core = 1 - core
    usable_block = usable_for(rows, sequences * tokens, tokens, heads_here, sequences)
    usable_summary = usable_for(rows, slots, slots // sequences, heads_here, sequences)
    lane = lax.broadcasted_iota(jnp.int32, (rows, width), 1)
    heads = [lax.rem(chip + (chips - step), chips) * 2 + core for step in range(chips)]
    key_parts, value_parts = [], []
    for head in heads:
        key_parts += [summary_keys_ref[head], keys_ref[head].reshape(sequences * tokens, width)]
        value_parts += [summary_values_ref[head], values_ref[head].reshape(sequences * tokens, width)]
    scores = [
        lax.dot_general(query_ref[i // 2], keys, (((1,), (1,)), ((), ())), preferred_element_type=jnp.float32)
        for i, keys in enumerate(key_parts)
    ]
    scores = [
        jnp.where(usable_block if i % 2 else usable_summary, score * scaling, VERY_NEGATIVE)
        for i, score in enumerate(scores)
    ]
    tops = [jnp.max(score, axis=-1, keepdims=True) for score in scores]
    exponents = [jnp.exp(score - top) for score, top in zip(scores, tops)]
    numerators = [
        lax.dot_general(
            exponent.astype(jnp.bfloat16), values, (((1,), (0,)), ((), ())), preferred_element_type=jnp.float32
        )
        for exponent, values in zip(exponents, value_parts)
    ]
    totals = [jnp.sum(exponent, axis=-1, keepdims=True) for exponent in exponents]
    for step in range(chips):
        l, s = 2 * step, 2 * step + 1
        stats = jnp.where(lane == 2, tops[s], totals[s])
        stats = jnp.where(lane == 0, tops[l], jnp.where(lane == 1, totals[l], stats))
        out_ref[step, :rows, :] = numerators[l]
        out_ref[step, rows : 2 * rows, :] = numerators[s]
        out_ref[step, 2 * rows :, :] = stats


def half(query, keys, values, summary_keys, summary_values, heads_here, flip):
    chips, rows, width = query.shape
    return pl.pallas_call(
        functools.partial(half_kernel, heads_here=heads_here, flip=flip),
        out_shape=jax.ShapeDtypeStruct((chips, 3 * rows, width), jnp.float32),
        in_specs=[pl.BlockSpec(memory_space=VMEM)] * 5,
        out_specs=pl.BlockSpec(memory_space=VMEM),
        cost_estimate=pl.CostEstimate(flops=10**8, transcendentals=10**5, bytes_accessed=10**6),
        compiler_params=pltpu.CompilerParams(vmem_limit_bytes=LIMIT),
        name="other_half" if flip else "own_half",
    )(query, keys, values, summary_keys, summary_values)


def join_kernel(own_ref, other_ref, told_ref, *out_refs, silent):
    chips, rows3, width = own_ref.shape
    told = jnp.where(lax.axis_index("shard") // 2 == silent, 0.0, told_ref[...].astype(jnp.float32)).astype(jnp.bfloat16)
    rows = rows3 // 3
    lane = lax.broadcasted_iota(jnp.int32, (rows, width), 1)
    for step in range(chips):
        out_ref = out_refs[step]
        own_stats = own_ref[step, 2 * rows :, :]
        other_stats = other_ref[step, 2 * rows :, :]
        stats = jnp.zeros((rows, width), jnp.float32)
        at = 0
        for branch in range(2):
            here = slice(branch * rows, (branch + 1) * rows)
            own_top, other_top = own_stats[:, 2 * branch : 2 * branch + 1], other_stats[:, 2 * branch : 2 * branch + 1]
            own_sum, other_sum = own_stats[:, 2 * branch + 1 : 2 * branch + 2], other_stats[:, 2 * branch + 1 : 2 * branch + 2]
            highest = jnp.maximum(own_top, other_top)
            own_weight, other_weight = jnp.exp(own_top - highest), jnp.exp(other_top - highest)
            numerator = own_weight * own_ref[step, here, :] + other_weight * other_ref[step, here, :]
            out_ref[here, :] = numerator.astype(jnp.bfloat16)
            for value in (highest, own_weight * own_sum + other_weight * other_sum):
                for term in split3(value):
                    stats = jnp.where(lane == at, term, stats)
                    at += 1
        out_ref[2 * rows : 3 * rows, :] = stats.astype(jnp.bfloat16)
        out_ref[3 * rows :, :] = told


def join(own, other, told, silent):
    chips, rows3, width = own.shape
    shape = jax.ShapeDtypeStruct((rows3 + told.shape[0], width), jnp.bfloat16)
    return pl.pallas_call(
        functools.partial(join_kernel, silent=silent),
        out_shape=[shape] * chips,
        in_specs=[pl.BlockSpec(memory_space=VMEM)] * 3,
        out_specs=[pl.BlockSpec(memory_space=VMEM)] * chips,
        compiler_params=pltpu.CompilerParams(vmem_limit_bytes=LIMIT),
        name="join",
    )(own, other, told)


def finish_kernel(*refs):
    *part_refs, gates_ref, counts_ref, out_ref, counts_out = refs
    rows, width = out_ref.shape
    _, sequences, heads_here = gates_ref.shape
    counts = counts_ref[...].astype(jnp.float32) + sum(ref[3 * rows :, :].astype(jnp.float32) for ref in part_refs)
    counts_out[...] = counts[: counts_out.shape[0]]
    row = lax.broadcasted_iota(jnp.int32, (rows, heads_here), 0)
    column = lax.broadcasted_iota(jnp.int32, (rows, heads_here), 1)
    stats = []
    for ref in part_refs:
        raw = ref[2 * rows : 3 * rows, :].astype(jnp.float32)
        stats.append([raw[:, i : i + 1] + raw[:, i + 1 : i + 2] + raw[:, i + 2 : i + 3] for i in (0, 3, 6, 9)])
    result = jnp.zeros((rows, width), jnp.float32)
    for branch in range(2):
        highest = functools.reduce(jnp.maximum, [s[2 * branch] for s in stats])
        weights = [jnp.exp(s[2 * branch] - highest) for s in stats]
        total = sum(weight * s[2 * branch + 1] for weight, s in zip(weights, stats))
        here = slice(branch * rows, (branch + 1) * rows)
        numerator = sum(weight * ref[here, :].astype(jnp.float32) for weight, ref in zip(weights, part_refs))
        gate = 1.0 / (1.0 + jnp.exp(-gates_ref[branch]))
        spread = jnp.zeros((rows, heads_here), jnp.float32)
        for sequence in range(sequences):
            spread = jnp.where(row // heads_here == sequence, gate[sequence : sequence + 1, :], spread)
        spread = jnp.sum(jnp.where(column == row % heads_here, spread, 0.0), axis=1, keepdims=True)
        result += numerator * (spread / total)
    out_ref[...] = result


def finish(parts, gates, counts, rows, count_rows):
    width = parts[0].shape[1]
    return pl.pallas_call(
        finish_kernel,
        out_shape=(
            jax.ShapeDtypeStruct((rows, width), jnp.float32),
            jax.ShapeDtypeStruct((count_rows, width), jnp.float32),
        ),
        in_specs=[pl.BlockSpec(memory_space=VMEM)] * (len(parts) + 2),
        out_specs=(pl.BlockSpec(memory_space=VMEM),) * 2,
        compiler_params=pltpu.CompilerParams(vmem_limit_bytes=LIMIT),
        name="finish",
    )(*parts, gates, counts)


def by_chips(queries, keys_cache, values_cache, summary_keys, summary_values, gate_logits, block_group_row, picked):
    groups, shards = lax.axis_size("grp"), lax.axis_size("shard")
    chips = shards // 2
    sequences, heads_here, width = queries.shape
    blocks = block_group_row.shape[1]
    rows = sequences * heads_here

    def shift(step):
        return [(s, (s // 2 + step) % chips * 2 + s % 2) for s in range(shards)]

    partner = [(s, s ^ 1) for s in range(shards)]
    mine = queries.reshape(rows, width)
    arrived = []
    for step in range(1, chips):
        arrived.append(lax.ppermute(mine, "shard", shift(step)))
    keys, values, counts, _ = fetch(block_group_row, picked, keys_cache, values_cache, True)
    offsets = [groups - 1 if chip == groups - 1 else chip + 1 if chip < groups - 2 else 1 for chip in range(chips)]
    pairs = [
        ((group ^ offsets[shard // 2]) * shards + shard, group * shards + shard)
        for group in range(groups)
        for shard in range(shards)
    ]
    told = lax.ppermute(counts, ("grp", "shard"), pairs)
    own_query = jnp.stack([mine] + arrived)
    other_query = lax.ppermute(own_query, "shard", partner)
    own = half(own_query, keys, values, summary_keys, summary_values, heads_here, False)
    other = half(other_query, keys, values, summary_keys, summary_values, heads_here, True)
    other = lax.ppermute(other, "shard", partner)
    parts = list(join(own, other, told, groups - 2))
    for step in range(1, chips):
        parts[step] = lax.ppermute(parts[step], "shard", shift(-step))
    attention, retrieval_counts = finish(parts, gate_logits, counts, rows, blocks // width)
    return attention.reshape(sequences, heads_here, width), retrieval_counts.reshape(-1)


def body(
    queries,
    paged_key_cache,
    paged_value_cache,
    summary_keys,
    summary_values,
    gate_logits,
    block_group_row,
    picked,
):
    groups, shards = lax.axis_size("grp"), lax.axis_size("shard")
    sequences, heads_here, width = queries.shape
    key_heads, _, picks = picked.shape
    blocks = block_group_row.shape[1]
    rows = sequences * heads_here
    always = shards == picks
    if shards == key_heads == picks and shards == 2 * groups and groups & (groups - 1) == 0:
        return by_chips(
            queries, paged_key_cache, paged_value_cache, summary_keys, summary_values, gate_logits, block_group_row, picked
        )

    keys, values, counts, valid = fetch(block_group_row, picked, paged_key_cache, paged_value_cache, always)
    tellers = groups - 1
    pairs = [
        ((group + 1 + shard) % groups * shards + shard, group * shards + shard)
        for group in range(groups)
        for shard in range(tellers)
    ]
    told = lax.ppermute(counts, ("grp", "shard"), pairs)

    copies = jnp.broadcast_to(queries.reshape(1, rows, width), (shards, rows, width))
    everyone = lax.all_to_all(copies, "shard", split_axis=0, concat_axis=0, tiled=True)
    everyone = everyone.reshape(key_heads, shards * rows // key_heads, width)
    outgoing = partials(everyone, keys, values, summary_keys, summary_values, told, valid, shards, heads_here)
    incoming = lax.all_to_all(outgoing, "shard", split_axis=0, concat_axis=0, tiled=True)
    attention, retrieval_counts = merge(incoming, gate_logits, counts, blocks // width, tellers)
    return attention.reshape(sequences, heads_here, width), retrieval_counts.reshape(-1)


def solution(mesh):
    placed = (
        P("grp", "shard", None),
        P(("grp", "shard"), None, None, None),
        P(("grp", "shard"), None, None, None),
        P(None, ("grp", "shard"), None),
        P(None, ("grp", "shard"), None),
        P(None, "grp", "shard"),
        P("grp", None),
        P(None, "grp", None),
    )
    return jax.shard_map(
        body, mesh=mesh, in_specs=placed, out_specs=(P("grp", "shard", None), P()), check_vma=False
    )
```

```python
import functools

import jax
import jax.numpy as jnp
from jax import lax
from jax.experimental import pallas as pl
from jax.experimental.pallas import tpu as pltpu
from jax.sharding import PartitionSpec as P


VERY_NEGATIVE = -1e30
VMEM = pltpu.VMEM
SMEM = pltpu.SMEM
LIMIT = 4 * 1024 * 1024


def fetch_kernel(rows_hbm, picked_hbm, keys_hbm, values_hbm, keys_out, values_out, counts_out, *refs, slots_here, blocks_each, with_valid):
    valid_out = refs[0] if with_valid else None
    sequences, blocks = rows_hbm.shape
    *rows_refs, picked_ref, picked_tile, rows_sem, picked_sem, tile_sem, key_sem, value_sem = refs[-7 - sequences :]
    copies = [pltpu.make_async_copy(rows_hbm.at[i], ref, rows_sem.at[i]) for i, ref in enumerate(rows_refs)]
    copies.append(pltpu.make_async_copy(picked_hbm, picked_ref, picked_sem))
    copies.append(pltpu.make_async_copy(picked_hbm, picked_tile, tile_sem))
    for copy in copies:
        copy.start()
    key_heads, _, picks = picked_ref.shape
    first = lax.axis_index("shard") * slots_here
    for copy in copies[:-1]:
        copy.wait()
    for head in range(key_heads):
        for sequence in range(sequences):
            places = []
            for pick in range(picks):
                slot = rows_refs[sequence][picked_ref[head, sequence, pick]]
                if slots_here & (slots_here - 1) == 0:
                    places.append(slot ^ first)
                else:
                    places.append(jnp.where(slot >= first, slot - first, slots_here))
            while len(places) > 1:
                places = [functools.reduce(jnp.minimum, places[i : i + 2]) for i in range(0, len(places), 2)]
            place = places[0]
            if valid_out is not None:
                found = place < slots_here
                valid_out[head, sequence] = found.astype(jnp.int32)
                place = jnp.where(found, place, sequence * blocks_each)
            pltpu.make_async_copy(keys_hbm.at[place, head], keys_out.at[head, sequence], key_sem).start()
            pltpu.make_async_copy(values_hbm.at[place, head], values_out.at[head, sequence], value_sem).start()
    copies[-1].wait()
    told_rows, width = counts_out.shape
    counts = []
    for row in range(told_rows):
        sums = [jnp.zeros((sequences, width), jnp.float32) for _ in range(2)]
        if row * width < blocks:
            block_ids = lax.broadcasted_iota(jnp.int32, (sequences, width), 1) + row * width
            for head in range(key_heads):
                tile = picked_tile[head]
                for pick in range(picks):
                    sums[pick % 2] += jnp.where(tile[:, pick : pick + 1] == block_ids, 1.0, 0.0)
        counts.append(jnp.sum(sums[0] + sums[1], axis=0, keepdims=True))
    counts_out[...] = jnp.concatenate(counts, axis=0).astype(jnp.bfloat16)
    pltpu.make_async_copy(keys_out, keys_out, key_sem).wait()
    pltpu.make_async_copy(values_out, values_out, value_sem).wait()


def fetch(block_group_row, picked, keys, values, always):
    key_heads, sequences, _ = picked.shape
    slots_here, _, tokens, width = keys.shape
    gathered = jax.ShapeDtypeStruct((key_heads, sequences, tokens, width), keys.dtype)
    told_rows = -(-block_group_row.shape[1] // (8 * width)) * 8
    nbytes = 2 * key_heads * sequences * tokens * width * 2
    out_shape = [gathered, gathered, jax.ShapeDtypeStruct((told_rows, width), jnp.bfloat16)]
    out_specs = [pl.BlockSpec(memory_space=VMEM)] * 3
    if not always:
        out_shape.append(jax.ShapeDtypeStruct((key_heads, sequences), jnp.int32))
        out_specs.append(pl.BlockSpec(memory_space=SMEM))
    out = pl.pallas_call(
        functools.partial(
            fetch_kernel, slots_here=slots_here, blocks_each=slots_here // sequences, with_valid=not always
        ),
        out_shape=out_shape,
        in_specs=[pl.BlockSpec(memory_space=pltpu.HBM)] * 4,
        out_specs=out_specs,
        scratch_shapes=[SMEM(block_group_row.shape[1:], jnp.int32)] * sequences
        + [SMEM(picked.shape, jnp.int32), VMEM(picked.shape, jnp.int32), pltpu.SemaphoreType.DMA((sequences,))]
        + [pltpu.SemaphoreType.DMA] * 4,
        cost_estimate=pl.CostEstimate(flops=0, transcendentals=0, bytes_accessed=2 * nbytes),
        compiler_params=pltpu.CompilerParams(vmem_limit_bytes=LIMIT),
        name="fetch",
    )(*(pltpu.with_memory_space_constraint(x, pltpu.HBM) for x in (block_group_row, picked, keys, values)))
    return out[0], out[1], out[2], None if always else out[3]


def split3(x):
    high = x.astype(jnp.bfloat16).astype(jnp.float32)
    rest = x - high
    middle = rest.astype(jnp.bfloat16).astype(jnp.float32)
    return high, middle, rest - middle


def attend_part(query, keys, values, usable, present):
    scaling = query.shape[-1] ** -0.5
    scores = lax.dot_general(query, keys, (((1,), (1,)), ((), ())), preferred_element_type=jnp.float32) * scaling
    scores = jnp.where(usable, scores, VERY_NEGATIVE)
    highest = jnp.max(scores, axis=-1, keepdims=True)
    exponent = jnp.exp(scores - highest)
    if present is not None:
        exponent = jnp.where(present, exponent, 0.0)
    total = jnp.sum(exponent, axis=-1, keepdims=True)
    numerator = lax.dot_general(
        exponent.astype(jnp.bfloat16), values, (((1,), (0,)), ((), ())), preferred_element_type=jnp.float32
    )
    return highest, total, numerator


def usable_for(rows, columns, each, heads_here, sequences):
    row = lax.broadcasted_iota(jnp.int32, (rows, columns), 0)
    column = lax.broadcasted_iota(jnp.int32, (rows, columns), 1)
    return (row // heads_here) % sequences == column // each


def partial_kernel(query_ref, keys_ref, values_ref, summary_keys_ref, summary_values_ref, told_ref, *refs, heads_here):
    valid_ref = refs[0] if len(refs) == 2 else None
    out_ref = refs[-1]
    key_heads, rows, width = query_ref.shape
    _, sequences, tokens, _ = keys_ref.shape
    slots = summary_keys_ref.shape[1]
    shards, sent_rows, _ = out_ref.shape
    told_rows = told_ref.shape[0]
    out_rows = (sent_rows - told_rows) // 3
    per_head = rows // out_rows

    usable_block = usable_for(rows, sequences * tokens, tokens, heads_here, sequences)
    usable_summary = usable_for(rows, slots, slots // sequences, heads_here, sequences)
    lane = lax.broadcasted_iota(jnp.int32, (rows, width), 1)
    for shard in range(shards):
        out_ref[shard, 3 * out_rows :, :] = told_ref[...]
    for head in range(key_heads):
        query = query_ref[head]
        present = None
        usable = usable_block
        if valid_ref is not None:
            column = lax.broadcasted_iota(jnp.int32, (rows, sequences * tokens), 1) // tokens
            flag = jnp.zeros((rows, sequences * tokens), jnp.int32)
            for sequence in range(sequences):
                flag = jnp.where(column == sequence, valid_ref[head, sequence], flag)
            usable = usable_block & (flag > 0)
            present = usable
        keys = keys_ref[head].reshape(sequences * tokens, width)
        values = values_ref[head].reshape(sequences * tokens, width)
        top_s, sum_s, num_s = attend_part(query, keys, values, usable, present)
        top_l, sum_l, num_l = attend_part(query, summary_keys_ref[head], summary_values_ref[head], usable_summary, None)
        stats = jnp.zeros((rows, width), jnp.float32)
        at = 0
        for value in (top_l, sum_l, top_s, sum_s):
            for term in split3(value):
                stats = jnp.where(lane == at, term, stats)
                at += 1
        for part in range(per_head):
            here = slice(part * out_rows, (part + 1) * out_rows)
            target = head * per_head + part
            for i, piece in enumerate((num_l, num_s, stats)):
                out_ref[target, i * out_rows : (i + 1) * out_rows, :] = piece[here].astype(jnp.bfloat16)


def partials(query, keys, values, summary_keys, summary_values, told, valid, shards, heads_here):
    key_heads, rows, width = query.shape
    out_rows = key_heads * rows // shards
    operands = [query, keys, values, summary_keys, summary_values, told]
    in_specs = [pl.BlockSpec(memory_space=VMEM)] * 6
    if valid is not None:
        operands.append(valid)
        in_specs.append(pl.BlockSpec(memory_space=SMEM))
    return pl.pallas_call(
        functools.partial(partial_kernel, heads_here=heads_here),
        out_shape=jax.ShapeDtypeStruct((shards, 3 * out_rows + told.shape[0], width), jnp.bfloat16),
        in_specs=in_specs,
        out_specs=pl.BlockSpec(memory_space=VMEM),
        compiler_params=pltpu.CompilerParams(vmem_limit_bytes=LIMIT),
        name="partials",
    )(*operands)


def merge_kernel(parts_ref, gates_ref, counts_ref, out_ref, counts_out, *, tellers):
    sources, sent_rows, width = parts_ref.shape
    told_rows = counts_ref.shape[0]
    rows = (sent_rows - told_rows) // 3
    _, sequences, heads_here = gates_ref.shape
    counts = counts_ref[...].astype(jnp.float32)
    for teller in range(tellers):
        counts += parts_ref[teller, 3 * rows :, :].astype(jnp.float32)
    counts_out[...] = counts[: counts_out.shape[0]]
    stats = []
    for source in range(sources):
        raw = parts_ref[source, 2 * rows : 3 * rows, :].astype(jnp.float32)
        stats.append([raw[:, i : i + 1] + raw[:, i + 1 : i + 2] + raw[:, i + 2 : i + 3] for i in (0, 3, 6, 9)])
    row = lax.broadcasted_iota(jnp.int32, (rows, heads_here), 0)
    column = lax.broadcasted_iota(jnp.int32, (rows, heads_here), 1)
    result = None
    for branch in range(2):
        highest = functools.reduce(jnp.maximum, [s[2 * branch] for s in stats])
        total = jnp.zeros((rows, 1), jnp.float32)
        numerator = jnp.zeros((rows, width), jnp.float32)
        for source in range(sources):
            weight = jnp.exp(stats[source][2 * branch] - highest)
            total += weight * stats[source][2 * branch + 1]
            numerator += weight * parts_ref[source, branch * rows : (branch + 1) * rows, :].astype(jnp.float32)
        gate = 1.0 / (1.0 + jnp.exp(-gates_ref[branch]))
        spread = jnp.zeros((rows, heads_here), jnp.float32)
        for sequence in range(sequences):
            spread = jnp.where(row // heads_here == sequence, gate[sequence : sequence + 1, :], spread)
        spread = jnp.sum(jnp.where(column == row % heads_here, spread, 0.0), axis=1, keepdims=True)
        term = numerator * (spread / total)
        result = term if result is None else result + term
    out_ref[...] = result


def merge(parts, gates, counts, count_rows, tellers):
    rows = (parts.shape[1] - counts.shape[0]) // 3
    width = parts.shape[2]
    return pl.pallas_call(
        functools.partial(merge_kernel, tellers=tellers),
        out_shape=(
            jax.ShapeDtypeStruct((rows, width), jnp.float32),
            jax.ShapeDtypeStruct((count_rows, width), jnp.float32),
        ),
        in_specs=[pl.BlockSpec(memory_space=VMEM)] * 3,
        out_specs=(pl.BlockSpec(memory_space=VMEM),) * 2,
        compiler_params=pltpu.CompilerParams(vmem_limit_bytes=LIMIT),
        name="merge",
    )(parts, gates, counts)


def half_kernel(query_ref, keys_ref, values_ref, summary_keys_ref, summary_values_ref, out_ref, *, heads_here, flip):
    chips, rows, width = query_ref.shape
    _, sequences, tokens, _ = keys_ref.shape
    slots = summary_keys_ref.shape[1]
    scaling = width**-0.5
    me = lax.axis_index("shard")
    chip, core = me // 2, me % 2
    if flip:
        core = 1 - core
    usable_block = usable_for(rows, sequences * tokens, tokens, heads_here, sequences)
    usable_summary = usable_for(rows, slots, slots // sequences, heads_here, sequences)
    lane = lax.broadcasted_iota(jnp.int32, (rows, width), 1)
    heads = [lax.rem(chip + (chips - step), chips) * 2 + (1 - core if step else core) for step in range(chips)]
    key_parts, value_parts = [], []
    for head in heads:
        key_parts += [summary_keys_ref[head], keys_ref[head].reshape(sequences * tokens, width)]
        value_parts += [summary_values_ref[head], values_ref[head].reshape(sequences * tokens, width)]
    scores = [
        lax.dot_general(query_ref[i // 2], keys, (((1,), (1,)), ((), ())), preferred_element_type=jnp.float32)
        for i, keys in enumerate(key_parts)
    ]
    scores = [
        jnp.where(usable_block if i % 2 else usable_summary, score * scaling, VERY_NEGATIVE)
        for i, score in enumerate(scores)
    ]
    tops = [jnp.max(score, axis=-1, keepdims=True) for score in scores]
    exponents = [jnp.exp(score - top) for score, top in zip(scores, tops)]
    numerators = [
        lax.dot_general(
            exponent.astype(jnp.bfloat16), values, (((1,), (0,)), ((), ())), preferred_element_type=jnp.float32
        )
        for exponent, values in zip(exponents, value_parts)
    ]
    totals = [jnp.sum(exponent, axis=-1, keepdims=True) for exponent in exponents]
    for step in range(chips):
        l, s = 2 * step, 2 * step + 1
        stats = jnp.where(lane == 2, tops[s], totals[s])
        stats = jnp.where(lane == 0, tops[l], jnp.where(lane == 1, totals[l], stats))
        out_ref[step, :rows, :] = numerators[l]
        out_ref[step, rows : 2 * rows, :] = numerators[s]
        out_ref[step, 2 * rows :, :] = stats


def half(query, keys, values, summary_keys, summary_values, heads_here, flip):
    chips, rows, width = query.shape
    return pl.pallas_call(
        functools.partial(half_kernel, heads_here=heads_here, flip=flip),
        out_shape=jax.ShapeDtypeStruct((chips, 3 * rows, width), jnp.float32),
        in_specs=[pl.BlockSpec(memory_space=VMEM)] * 5,
        out_specs=pl.BlockSpec(memory_space=VMEM),
        cost_estimate=pl.CostEstimate(flops=10**8, transcendentals=10**5, bytes_accessed=10**6),
        compiler_params=pltpu.CompilerParams(vmem_limit_bytes=LIMIT),
        name="other_half" if flip else "own_half",
    )(query, keys, values, summary_keys, summary_values)


def join_kernel(own_ref, other_ref, told_ref, *out_refs, silent):
    chips, rows3, width = own_ref.shape
    told = jnp.where(lax.axis_index("shard") // 2 == silent, 0.0, told_ref[...].astype(jnp.float32)).astype(jnp.bfloat16)
    rows = rows3 // 3
    lane = lax.broadcasted_iota(jnp.int32, (rows, width), 1)
    for step in range(chips):
        out_ref = out_refs[step]
        own_stats = own_ref[step, 2 * rows :, :]
        other_stats = other_ref[step, 2 * rows :, :]
        stats = jnp.zeros((rows, width), jnp.float32)
        at = 0
        for branch in range(2):
            here = slice(branch * rows, (branch + 1) * rows)
            own_top, other_top = own_stats[:, 2 * branch : 2 * branch + 1], other_stats[:, 2 * branch : 2 * branch + 1]
            own_sum, other_sum = own_stats[:, 2 * branch + 1 : 2 * branch + 2], other_stats[:, 2 * branch + 1 : 2 * branch + 2]
            highest = jnp.maximum(own_top, other_top)
            own_weight, other_weight = jnp.exp(own_top - highest), jnp.exp(other_top - highest)
            numerator = own_weight * own_ref[step, here, :] + other_weight * other_ref[step, here, :]
            out_ref[here, :] = numerator.astype(jnp.bfloat16)
            for value in (highest, own_weight * own_sum + other_weight * other_sum):
                for term in split3(value):
                    stats = jnp.where(lane == at, term, stats)
                    at += 1
        out_ref[2 * rows : 3 * rows, :] = stats.astype(jnp.bfloat16)
        out_ref[3 * rows :, :] = told


def join(own, other, told, silent):
    chips, rows3, width = own.shape
    shape = jax.ShapeDtypeStruct((rows3 + told.shape[0], width), jnp.bfloat16)
    return pl.pallas_call(
        functools.partial(join_kernel, silent=silent),
        out_shape=[shape] * chips,
        in_specs=[pl.BlockSpec(memory_space=VMEM)] * 3,
        out_specs=[pl.BlockSpec(memory_space=VMEM)] * chips,
        compiler_params=pltpu.CompilerParams(vmem_limit_bytes=LIMIT),
        name="join",
    )(own, other, told)


def finish_kernel(*refs):
    *part_refs, gates_ref, counts_ref, out_ref, counts_out = refs
    rows, width = out_ref.shape
    _, sequences, heads_here = gates_ref.shape
    counts = counts_ref[...].astype(jnp.float32) + sum(ref[3 * rows :, :].astype(jnp.float32) for ref in part_refs)
    counts_out[...] = counts[: counts_out.shape[0]]
    row = lax.broadcasted_iota(jnp.int32, (rows, heads_here), 0)
    column = lax.broadcasted_iota(jnp.int32, (rows, heads_here), 1)
    stats = []
    for ref in part_refs:
        raw = ref[2 * rows : 3 * rows, :].astype(jnp.float32)
        stats.append([raw[:, i : i + 1] + raw[:, i + 1 : i + 2] + raw[:, i + 2 : i + 3] for i in (0, 3, 6, 9)])
    result = jnp.zeros((rows, width), jnp.float32)
    for branch in range(2):
        highest = functools.reduce(jnp.maximum, [s[2 * branch] for s in stats])
        weights = [jnp.exp(s[2 * branch] - highest) for s in stats]
        total = sum(weight * s[2 * branch + 1] for weight, s in zip(weights, stats))
        here = slice(branch * rows, (branch + 1) * rows)
        numerator = sum(weight * ref[here, :].astype(jnp.float32) for weight, ref in zip(weights, part_refs))
        gate = 1.0 / (1.0 + jnp.exp(-gates_ref[branch]))
        spread = jnp.zeros((rows, heads_here), jnp.float32)
        for sequence in range(sequences):
            spread = jnp.where(row // heads_here == sequence, gate[sequence : sequence + 1, :], spread)
        spread = jnp.sum(jnp.where(column == row % heads_here, spread, 0.0), axis=1, keepdims=True)
        result += numerator * (spread / total)
    out_ref[...] = result


def finish(parts, gates, counts, rows, count_rows):
    width = parts[0].shape[1]
    return pl.pallas_call(
        finish_kernel,
        out_shape=(
            jax.ShapeDtypeStruct((rows, width), jnp.float32),
            jax.ShapeDtypeStruct((count_rows, width), jnp.float32),
        ),
        in_specs=[pl.BlockSpec(memory_space=VMEM)] * (len(parts) + 2),
        out_specs=(pl.BlockSpec(memory_space=VMEM),) * 2,
        compiler_params=pltpu.CompilerParams(vmem_limit_bytes=LIMIT),
        name="finish",
    )(*parts, gates, counts)


def by_chips(queries, keys_cache, values_cache, summary_keys, summary_values, gate_logits, block_group_row, picked):
    groups, shards = lax.axis_size("grp"), lax.axis_size("shard")
    chips = shards // 2
    sequences, heads_here, width = queries.shape
    blocks = block_group_row.shape[1]
    rows = sequences * heads_here

    def shift(step):
        return [(s, (s // 2 + step) % chips * 2 + 1 - s % 2) for s in range(shards)]

    partner = [(s, s ^ 1) for s in range(shards)]
    mine = queries.reshape(rows, width)
    arrived = []
    for step in range(1, chips):
        arrived.append(lax.ppermute(mine, "shard", shift(step)))
    keys, values, counts, _ = fetch(block_group_row, picked, keys_cache, values_cache, True)
    offsets = [groups - 1 if chip == groups - 1 else (chip + 1) % (groups - 1) for chip in range(chips)]
    pairs = [
        ((group ^ offsets[shard // 2]) * shards + (shard if offsets[shard // 2] else shard ^ 1), group * shards + shard)
        for group in range(groups)
        for shard in range(shards)
    ]
    told = lax.ppermute(counts, ("grp", "shard"), pairs)
    own_query = jnp.stack([mine] + arrived)
    other_query = lax.ppermute(own_query, "shard", partner)
    own = half(own_query, keys, values, summary_keys, summary_values, heads_here, False)
    other = half(other_query, keys, values, summary_keys, summary_values, heads_here, True)
    other = lax.ppermute(other, "shard", partner)
    parts = list(join(own, other, told, groups - 2))
    for step in range(1, chips):
        parts[step] = lax.ppermute(parts[step], "shard", shift(-step))
    attention, retrieval_counts = finish(parts, gate_logits, counts, rows, blocks // width)
    return attention.reshape(sequences, heads_here, width), retrieval_counts.reshape(-1)


def body(
    queries,
    paged_key_cache,
    paged_value_cache,
    summary_keys,
    summary_values,
    gate_logits,
    block_group_row,
    picked,
):
    groups, shards = lax.axis_size("grp"), lax.axis_size("shard")
    sequences, heads_here, width = queries.shape
    key_heads, _, picks = picked.shape
    blocks = block_group_row.shape[1]
    rows = sequences * heads_here
    always = shards == picks
    if shards == key_heads == picks and shards == 2 * groups and groups & (groups - 1) == 0:
        return by_chips(
            queries, paged_key_cache, paged_value_cache, summary_keys, summary_values, gate_logits, block_group_row, picked
        )

    keys, values, counts, valid = fetch(block_group_row, picked, paged_key_cache, paged_value_cache, always)
    tellers = groups - 1
    pairs = [
        ((group + 1 + shard) % groups * shards + shard, group * shards + shard)
        for group in range(groups)
        for shard in range(tellers)
    ]
    told = lax.ppermute(counts, ("grp", "shard"), pairs)

    copies = jnp.broadcast_to(queries.reshape(1, rows, width), (shards, rows, width))
    everyone = lax.all_to_all(copies, "shard", split_axis=0, concat_axis=0, tiled=True)
    everyone = everyone.reshape(key_heads, shards * rows // key_heads, width)
    outgoing = partials(everyone, keys, values, summary_keys, summary_values, told, valid, shards, heads_here)
    incoming = lax.all_to_all(outgoing, "shard", split_axis=0, concat_axis=0, tiled=True)
    attention, retrieval_counts = merge(incoming, gate_logits, counts, blocks // width, tellers)
    return attention.reshape(sequences, heads_here, width), retrieval_counts.reshape(-1)


def solution(mesh):
    placed = (
        P("grp", "shard", None),
        P(("grp", "shard"), None, None, None),
        P(("grp", "shard"), None, None, None),
        P(None, ("grp", "shard"), None),
        P(None, ("grp", "shard"), None),
        P(None, "grp", "shard"),
        P("grp", None),
        P(None, "grp", None),
    )
    return jax.shard_map(
        body, mesh=mesh, in_specs=placed, out_specs=(P("grp", "shard", None), P()), check_vma=False
    )
```

```python
import functools

import jax
import jax.numpy as jnp
from jax import lax
from jax.experimental import pallas as pl
from jax.experimental.pallas import tpu as pltpu
from jax.sharding import PartitionSpec as P


VERY_NEGATIVE = -1e30
VMEM = pltpu.VMEM
SMEM = pltpu.SMEM
LIMIT = 4 * 1024 * 1024


def fetch_kernel(rows_hbm, picked_hbm, keys_hbm, values_hbm, keys_out, values_out, counts_out, *refs, slots_here, blocks_each, with_valid):
    valid_out = refs[0] if with_valid else None
    sequences, blocks = rows_hbm.shape
    *rows_refs, picked_ref, picked_tile, rows_sem, picked_sem, tile_sem, key_sem, value_sem = refs[-7 - sequences :]
    copies = [pltpu.make_async_copy(rows_hbm.at[i], ref, rows_sem.at[i]) for i, ref in enumerate(rows_refs)]
    copies.append(pltpu.make_async_copy(picked_hbm, picked_ref, picked_sem))
    copies.append(pltpu.make_async_copy(picked_hbm, picked_tile, tile_sem))
    for copy in copies:
        copy.start()
    key_heads, _, picks = picked_ref.shape
    first = lax.axis_index("shard") * slots_here
    for copy in copies[:-1]:
        copy.wait()
    for head in range(key_heads):
        for sequence in range(sequences):
            places = []
            for pick in range(picks):
                slot = rows_refs[sequence][picked_ref[head, sequence, pick]]
                if slots_here & (slots_here - 1) == 0:
                    places.append(slot ^ first)
                else:
                    places.append(jnp.where(slot >= first, slot - first, slots_here))
            while len(places) > 1:
                places = [functools.reduce(jnp.minimum, places[i : i + 2]) for i in range(0, len(places), 2)]
            place = places[0]
            if valid_out is not None:
                found = place < slots_here
                valid_out[head, sequence] = found.astype(jnp.int32)
                place = jnp.where(found, place, sequence * blocks_each)
            elif slots_here & (slots_here - 1) == 0:
                place = place & (slots_here - 1)
            pltpu.make_async_copy(keys_hbm.at[place, head], keys_out.at[head, sequence], key_sem).start()
            pltpu.make_async_copy(values_hbm.at[place, head], values_out.at[head, sequence], value_sem).start()
    copies[-1].wait()
    told_rows, width = counts_out.shape
    counts = []
    for row in range(told_rows):
        sums = [jnp.zeros((sequences, width), jnp.float32) for _ in range(2)]
        if row * width < blocks:
            block_ids = lax.broadcasted_iota(jnp.int32, (sequences, width), 1) + row * width
            for head in range(key_heads):
                tile = picked_tile[head]
                for pick in range(picks):
                    sums[pick % 2] += jnp.where(tile[:, pick : pick + 1] == block_ids, 1.0, 0.0)
        counts.append(jnp.sum(sums[0] + sums[1], axis=0, keepdims=True))
    counts_out[...] = jnp.concatenate(counts, axis=0).astype(jnp.bfloat16)
    pltpu.make_async_copy(keys_out, keys_out, key_sem).wait()
    pltpu.make_async_copy(values_out, values_out, value_sem).wait()


def fetch(block_group_row, picked, keys, values, always):
    key_heads, sequences, _ = picked.shape
    slots_here, _, tokens, width = keys.shape
    gathered = jax.ShapeDtypeStruct((key_heads, sequences, tokens, width), keys.dtype)
    told_rows = -(-block_group_row.shape[1] // (8 * width)) * 8
    nbytes = 2 * key_heads * sequences * tokens * width * 2
    out_shape = [gathered, gathered, jax.ShapeDtypeStruct((told_rows, width), jnp.bfloat16)]
    out_specs = [pl.BlockSpec(memory_space=VMEM)] * 3
    if not always:
        out_shape.append(jax.ShapeDtypeStruct((key_heads, sequences), jnp.int32))
        out_specs.append(pl.BlockSpec(memory_space=SMEM))
    out = pl.pallas_call(
        functools.partial(
            fetch_kernel, slots_here=slots_here, blocks_each=slots_here // sequences, with_valid=not always
        ),
        out_shape=out_shape,
        in_specs=[pl.BlockSpec(memory_space=pltpu.HBM)] * 4,
        out_specs=out_specs,
        scratch_shapes=[SMEM(block_group_row.shape[1:], jnp.int32)] * sequences
        + [SMEM(picked.shape, jnp.int32), VMEM(picked.shape, jnp.int32), pltpu.SemaphoreType.DMA((sequences,))]
        + [pltpu.SemaphoreType.DMA] * 4,
        cost_estimate=pl.CostEstimate(flops=0, transcendentals=0, bytes_accessed=2 * nbytes),
        compiler_params=pltpu.CompilerParams(vmem_limit_bytes=LIMIT),
        name="fetch",
    )(*(pltpu.with_memory_space_constraint(x, pltpu.HBM) for x in (block_group_row, picked, keys, values)))
    return out[0], out[1], out[2], None if always else out[3]


def split3(x):
    high = x.astype(jnp.bfloat16).astype(jnp.float32)
    rest = x - high
    middle = rest.astype(jnp.bfloat16).astype(jnp.float32)
    return high, middle, rest - middle


def attend_part(query, keys, values, usable, present):
    scaling = query.shape[-1] ** -0.5
    scores = lax.dot_general(query, keys, (((1,), (1,)), ((), ())), preferred_element_type=jnp.float32) * scaling
    scores = jnp.where(usable, scores, VERY_NEGATIVE)
    highest = jnp.max(scores, axis=-1, keepdims=True)
    exponent = jnp.exp(scores - highest)
    if present is not None:
        exponent = jnp.where(present, exponent, 0.0)
    total = jnp.sum(exponent, axis=-1, keepdims=True)
    numerator = lax.dot_general(
        exponent.astype(jnp.bfloat16), values, (((1,), (0,)), ((), ())), preferred_element_type=jnp.float32
    )
    return highest, total, numerator


def usable_for(rows, columns, each, heads_here, sequences):
    row = lax.broadcasted_iota(jnp.int32, (rows, columns), 0)
    column = lax.broadcasted_iota(jnp.int32, (rows, columns), 1)
    return (row // heads_here) % sequences == column // each


def partial_kernel(query_ref, keys_ref, values_ref, summary_keys_ref, summary_values_ref, told_ref, *refs, heads_here):
    valid_ref = refs[0] if len(refs) == 2 else None
    out_ref = refs[-1]
    key_heads, rows, width = query_ref.shape
    _, sequences, tokens, _ = keys_ref.shape
    slots = summary_keys_ref.shape[1]
    shards, sent_rows, _ = out_ref.shape
    told_rows = told_ref.shape[0]
    out_rows = (sent_rows - told_rows) // 3
    per_head = rows // out_rows

    usable_block = usable_for(rows, sequences * tokens, tokens, heads_here, sequences)
    usable_summary = usable_for(rows, slots, slots // sequences, heads_here, sequences)
    lane = lax.broadcasted_iota(jnp.int32, (rows, width), 1)
    for shard in range(shards):
        out_ref[shard, 3 * out_rows :, :] = told_ref[...]
    for head in range(key_heads):
        query = query_ref[head]
        present = None
        usable = usable_block
        if valid_ref is not None:
            column = lax.broadcasted_iota(jnp.int32, (rows, sequences * tokens), 1) // tokens
            flag = jnp.zeros((rows, sequences * tokens), jnp.int32)
            for sequence in range(sequences):
                flag = jnp.where(column == sequence, valid_ref[head, sequence], flag)
            usable = usable_block & (flag > 0)
            present = usable
        keys = keys_ref[head].reshape(sequences * tokens, width)
        values = values_ref[head].reshape(sequences * tokens, width)
        top_s, sum_s, num_s = attend_part(query, keys, values, usable, present)
        top_l, sum_l, num_l = attend_part(query, summary_keys_ref[head], summary_values_ref[head], usable_summary, None)
        stats = jnp.zeros((rows, width), jnp.float32)
        at = 0
        for value in (top_l, sum_l, top_s, sum_s):
            for term in split3(value):
                stats = jnp.where(lane == at, term, stats)
                at += 1
        for part in range(per_head):
            here = slice(part * out_rows, (part + 1) * out_rows)
            target = head * per_head + part
            for i, piece in enumerate((num_l, num_s, stats)):
                out_ref[target, i * out_rows : (i + 1) * out_rows, :] = piece[here].astype(jnp.bfloat16)


def partials(query, keys, values, summary_keys, summary_values, told, valid, shards, heads_here):
    key_heads, rows, width = query.shape
    out_rows = key_heads * rows // shards
    operands = [query, keys, values, summary_keys, summary_values, told]
    in_specs = [pl.BlockSpec(memory_space=VMEM)] * 6
    if valid is not None:
        operands.append(valid)
        in_specs.append(pl.BlockSpec(memory_space=SMEM))
    return pl.pallas_call(
        functools.partial(partial_kernel, heads_here=heads_here),
        out_shape=jax.ShapeDtypeStruct((shards, 3 * out_rows + told.shape[0], width), jnp.bfloat16),
        in_specs=in_specs,
        out_specs=pl.BlockSpec(memory_space=VMEM),
        compiler_params=pltpu.CompilerParams(vmem_limit_bytes=LIMIT),
        name="partials",
    )(*operands)


def merge_kernel(parts_ref, gates_ref, counts_ref, out_ref, counts_out, *, tellers):
    sources, sent_rows, width = parts_ref.shape
    told_rows = counts_ref.shape[0]
    rows = (sent_rows - told_rows) // 3
    _, sequences, heads_here = gates_ref.shape
    counts = counts_ref[...].astype(jnp.float32)
    for teller in range(tellers):
        counts += parts_ref[teller, 3 * rows :, :].astype(jnp.float32)
    counts_out[...] = counts[: counts_out.shape[0]]
    stats = []
    for source in range(sources):
        raw = parts_ref[source, 2 * rows : 3 * rows, :].astype(jnp.float32)
        stats.append([raw[:, i : i + 1] + raw[:, i + 1 : i + 2] + raw[:, i + 2 : i + 3] for i in (0, 3, 6, 9)])
    row = lax.broadcasted_iota(jnp.int32, (rows, heads_here), 0)
    column = lax.broadcasted_iota(jnp.int32, (rows, heads_here), 1)
    result = None
    for branch in range(2):
        highest = functools.reduce(jnp.maximum, [s[2 * branch] for s in stats])
        total = jnp.zeros((rows, 1), jnp.float32)
        numerator = jnp.zeros((rows, width), jnp.float32)
        for source in range(sources):
            weight = jnp.exp(stats[source][2 * branch] - highest)
            total += weight * stats[source][2 * branch + 1]
            numerator += weight * parts_ref[source, branch * rows : (branch + 1) * rows, :].astype(jnp.float32)
        gate = 1.0 / (1.0 + jnp.exp(-gates_ref[branch]))
        spread = jnp.zeros((rows, heads_here), jnp.float32)
        for sequence in range(sequences):
            spread = jnp.where(row // heads_here == sequence, gate[sequence : sequence + 1, :], spread)
        spread = jnp.sum(jnp.where(column == row % heads_here, spread, 0.0), axis=1, keepdims=True)
        term = numerator * (spread / total)
        result = term if result is None else result + term
    out_ref[...] = result


def merge(parts, gates, counts, count_rows, tellers):
    rows = (parts.shape[1] - counts.shape[0]) // 3
    width = parts.shape[2]
    return pl.pallas_call(
        functools.partial(merge_kernel, tellers=tellers),
        out_shape=(
            jax.ShapeDtypeStruct((rows, width), jnp.float32),
            jax.ShapeDtypeStruct((count_rows, width), jnp.float32),
        ),
        in_specs=[pl.BlockSpec(memory_space=VMEM)] * 3,
        out_specs=(pl.BlockSpec(memory_space=VMEM),) * 2,
        compiler_params=pltpu.CompilerParams(vmem_limit_bytes=LIMIT),
        name="merge",
    )(parts, gates, counts)


def half_kernel(query_ref, keys_ref, values_ref, summary_keys_ref, summary_values_ref, *refs, heads_here, flip):
    out_ref = refs[0] if flip else refs[1]
    chips, rows, width = query_ref.shape
    _, sequences, tokens, _ = keys_ref.shape
    slots = summary_keys_ref.shape[1]
    scaling = width**-0.5
    me = lax.axis_index("shard")
    chip, core = me // 2, me % 2
    if flip:
        core = 1 - core
    usable_block = usable_for(rows, sequences * tokens, tokens, heads_here, sequences)
    usable_summary = usable_for(rows, slots, slots // sequences, heads_here, sequences)
    lane = lax.broadcasted_iota(jnp.int32, (rows, width), 1)
    heads = [lax.rem(chip + (chips - step), chips) * 2 + (1 - core if step else core) for step in range(chips)]
    key_parts, value_parts = [], []
    for head in heads:
        key_parts += [summary_keys_ref[head], keys_ref[head].reshape(sequences * tokens, width)]
        value_parts += [summary_values_ref[head], values_ref[head].reshape(sequences * tokens, width)]
    scores = [
        lax.dot_general(query_ref[i // 2], keys, (((1,), (1,)), ((), ())), preferred_element_type=jnp.float32)
        for i, keys in enumerate(key_parts)
    ]
    scores = [
        jnp.where(usable_block if i % 2 else usable_summary, score * scaling, VERY_NEGATIVE)
        for i, score in enumerate(scores)
    ]
    tops = [jnp.max(score, axis=-1, keepdims=True) for score in scores]
    exponents = [jnp.exp(score - top) for score, top in zip(scores, tops)]
    numerators = [
        lax.dot_general(
            exponent.astype(jnp.bfloat16), values, (((1,), (0,)), ((), ())), preferred_element_type=jnp.float32
        )
        for exponent, values in zip(exponents, value_parts)
    ]
    totals = [jnp.sum(exponent, axis=-1, keepdims=True) for exponent in exponents]
    stats = jnp.zeros((rows, width), jnp.float32)
    for i, value in enumerate(tops + totals):
        stats = jnp.where(lane == i, value, stats)
    for i, numerator in enumerate(numerators):
        out_ref[i * rows : (i + 1) * rows, :] = numerator
    out_ref[2 * chips * rows :, :] = stats
    if not flip:
        gates_ref, gate_ref = refs[0], refs[2]
        row = lax.broadcasted_iota(jnp.int32, (rows, heads_here), 0)
        column = lax.broadcasted_iota(jnp.int32, (rows, heads_here), 1)
        tile = jnp.zeros((rows, width), jnp.float32)
        for branch in range(2):
            gate = 1.0 / (1.0 + jnp.exp(-gates_ref[branch]))
            spread = jnp.zeros((rows, heads_here), jnp.float32)
            for sequence in range(sequences):
                spread = jnp.where(row // heads_here == sequence, gate[sequence : sequence + 1, :], spread)
            spread = jnp.sum(jnp.where(column == row % heads_here, spread, 0.0), axis=1, keepdims=True)
            tile = jnp.where(lane == branch, spread, tile)
        gate_ref[...] = tile


def half(query, keys, values, summary_keys, summary_values, gates, heads_here, flip):
    chips, rows, width = query.shape
    operands = [query, keys, values, summary_keys, summary_values] + ([] if flip else [gates])
    out_shape = [jax.ShapeDtypeStruct(((2 * chips + 1) * rows, width), jnp.float32)]
    if not flip:
        out_shape.append(jax.ShapeDtypeStruct((rows, width), jnp.float32))
    return pl.pallas_call(
        functools.partial(half_kernel, heads_here=heads_here, flip=flip),
        out_shape=out_shape,
        in_specs=[pl.BlockSpec(memory_space=VMEM)] * len(operands),
        out_specs=[pl.BlockSpec(memory_space=VMEM)] * len(out_shape),
        cost_estimate=pl.CostEstimate(flops=10**8, transcendentals=10**5, bytes_accessed=10**6),
        compiler_params=pltpu.CompilerParams(vmem_limit_bytes=LIMIT),
        name="other_half" if flip else "own_half",
    )(*operands)


def lanes_down(x, count):
    return pltpu.roll(x, x.shape[1] - count, axis=1) if count else x


def lanes_up(x, count):
    return pltpu.roll(x, count, axis=1)


def join_kernel(own_ref, other_ref, told_ref, *out_refs, silent):
    chips = len(out_refs)
    parts = 2 * chips
    all_rows, width = own_ref.shape
    rows = all_rows // (parts + 1)
    told = jnp.where(lax.axis_index("shard") // 2 == silent, 0.0, told_ref[...].astype(jnp.float32)).astype(jnp.bfloat16)
    lane = lax.broadcasted_iota(jnp.int32, (rows, width), 1)
    own_stats, other_stats = own_ref[parts * rows :, :], other_ref[parts * rows :, :]
    highest = jnp.maximum(own_stats, other_stats)
    own_weight, other_weight = jnp.exp(own_stats - highest), jnp.exp(other_stats - highest)
    total = own_weight * lanes_down(own_stats, parts) + other_weight * lanes_down(other_stats, parts)
    stats = jnp.where(lane < parts, highest, jnp.where(lane < 2 * parts, lanes_up(total, parts), 0.0))
    high, middle, low = split3(stats)
    stats = (high + lanes_up(middle, 2 * parts) + lanes_up(low, 4 * parts)).astype(jnp.bfloat16)
    for i in range(parts):
        here, there = slice(i * rows, (i + 1) * rows), slice(i % 2 * rows, (i % 2 + 1) * rows)
        numerator = own_weight[:, i : i + 1] * own_ref[here, :] + other_weight[:, i : i + 1] * other_ref[here, :]
        out_refs[i // 2][there, :] = numerator.astype(jnp.bfloat16)
    for out_ref in out_refs:
        out_ref[2 * rows : 3 * rows, :] = stats
        out_ref[3 * rows :, :] = told


def join(own, other, told, chips, silent):
    all_rows, width = own.shape
    rows = all_rows // (2 * chips + 1)
    shape = jax.ShapeDtypeStruct((3 * rows + told.shape[0], width), jnp.bfloat16)
    return pl.pallas_call(
        functools.partial(join_kernel, silent=silent),
        out_shape=[shape] * chips,
        in_specs=[pl.BlockSpec(memory_space=VMEM)] * 3,
        out_specs=[pl.BlockSpec(memory_space=VMEM)] * chips,
        compiler_params=pltpu.CompilerParams(vmem_limit_bytes=LIMIT),
        name="join",
    )(own, other, told)


def finish_kernel(*refs):
    *part_refs, gate_ref, counts_ref, out_ref, counts_out = refs
    rows, width = out_ref.shape
    parts = 2 * len(part_refs)
    maxima, sums = [], []
    for step, ref in enumerate(part_refs):
        raw = ref[2 * rows : 3 * rows, :].astype(jnp.float32)
        for values, first in ((maxima, 2 * step), (sums, 2 * step + parts)):
            high, middle, low = (lanes_down(raw, first + 2 * parts * term) for term in range(3))
            values.append(high + middle + low)
    highest = functools.reduce(jnp.maximum, maxima)
    weights = [jnp.exp(value - highest) for value in maxima]
    share = gate_ref[...] / sum(weight * value for weight, value in zip(weights, sums))
    result = jnp.zeros((rows, width), jnp.float32)
    for weight, ref in zip(weights, part_refs):
        scaled = weight * share
        for branch in range(2):
            numerator = ref[branch * rows : (branch + 1) * rows, :].astype(jnp.float32)
            result += scaled[:, branch : branch + 1] * numerator
    out_ref[...] = result
    counts = counts_ref[...].astype(jnp.float32) + sum(ref[3 * rows :, :].astype(jnp.float32) for ref in part_refs)
    counts_out[...] = counts[: counts_out.shape[0]]


def finish(parts, gates, counts, rows, count_rows):
    width = parts[0].shape[1]
    return pl.pallas_call(
        finish_kernel,
        out_shape=(
            jax.ShapeDtypeStruct((rows, width), jnp.float32),
            jax.ShapeDtypeStruct((count_rows, width), jnp.float32),
        ),
        in_specs=[pl.BlockSpec(memory_space=VMEM)] * (len(parts) + 2),
        out_specs=(pl.BlockSpec(memory_space=VMEM),) * 2,
        compiler_params=pltpu.CompilerParams(vmem_limit_bytes=LIMIT),
        name="finish",
    )(*parts, gates, counts)


def by_chips(queries, keys_cache, values_cache, summary_keys, summary_values, gate_logits, block_group_row, picked):
    groups, shards = lax.axis_size("grp"), lax.axis_size("shard")
    chips = shards // 2
    sequences, heads_here, width = queries.shape
    blocks = block_group_row.shape[1]
    rows = sequences * heads_here

    def shift(step):
        return [(s, (s // 2 + step) % chips * 2 + 1 - s % 2) for s in range(shards)]

    partner = [(s, s ^ 1) for s in range(shards)]
    mine = queries.reshape(rows, width)
    arrived = []
    for step in range(1, chips):
        arrived.append(lax.ppermute(mine, "shard", shift(step)))
    keys, values, counts, _ = fetch(block_group_row, picked, keys_cache, values_cache, True)
    offsets = [groups - 1 if chip == groups - 1 else (chip + 1) % (groups - 1) for chip in range(chips)]
    pairs = [
        ((group ^ offsets[shard // 2]) * shards + (shard if offsets[shard // 2] else shard ^ 1), group * shards + shard)
        for group in range(groups)
        for shard in range(shards)
    ]
    told = lax.ppermute(counts, ("grp", "shard"), pairs)
    own_query = jnp.stack([mine] + arrived)
    other_query = lax.ppermute(own_query, "shard", partner)
    own, gates = half(own_query, keys, values, summary_keys, summary_values, gate_logits, heads_here, False)
    (other,) = half(other_query, keys, values, summary_keys, summary_values, None, heads_here, True)
    other = lax.ppermute(other, "shard", partner)
    parts = list(join(own, other, told, chips, groups - 2))
    for step in range(1, chips):
        parts[step] = lax.ppermute(parts[step], "shard", shift(-step))
    attention, retrieval_counts = finish(parts, gates, counts, rows, blocks // width)
    return attention.reshape(sequences, heads_here, width), retrieval_counts.reshape(-1)


def body(
    queries,
    paged_key_cache,
    paged_value_cache,
    summary_keys,
    summary_values,
    gate_logits,
    block_group_row,
    picked,
):
    groups, shards = lax.axis_size("grp"), lax.axis_size("shard")
    sequences, heads_here, width = queries.shape
    key_heads, _, picks = picked.shape
    blocks = block_group_row.shape[1]
    rows = sequences * heads_here
    always = shards == picks
    if shards == key_heads == picks and shards == 2 * groups and groups & (groups - 1) == 0 and 6 * shards <= width:
        return by_chips(
            queries, paged_key_cache, paged_value_cache, summary_keys, summary_values, gate_logits, block_group_row, picked
        )

    keys, values, counts, valid = fetch(block_group_row, picked, paged_key_cache, paged_value_cache, always)
    tellers = groups - 1
    pairs = [
        ((group + 1 + shard) % groups * shards + shard, group * shards + shard)
        for group in range(groups)
        for shard in range(tellers)
    ]
    told = lax.ppermute(counts, ("grp", "shard"), pairs)

    copies = jnp.broadcast_to(queries.reshape(1, rows, width), (shards, rows, width))
    everyone = lax.all_to_all(copies, "shard", split_axis=0, concat_axis=0, tiled=True)
    everyone = everyone.reshape(key_heads, shards * rows // key_heads, width)
    outgoing = partials(everyone, keys, values, summary_keys, summary_values, told, valid, shards, heads_here)
    incoming = lax.all_to_all(outgoing, "shard", split_axis=0, concat_axis=0, tiled=True)
    attention, retrieval_counts = merge(incoming, gate_logits, counts, blocks // width, tellers)
    return attention.reshape(sequences, heads_here, width), retrieval_counts.reshape(-1)


def solution(mesh):
    placed = (
        P("grp", "shard", None),
        P(("grp", "shard"), None, None, None),
        P(("grp", "shard"), None, None, None),
        P(None, ("grp", "shard"), None),
        P(None, ("grp", "shard"), None),
        P(None, "grp", "shard"),
        P("grp", None),
        P(None, "grp", None),
    )
    return jax.shard_map(
        body, mesh=mesh, in_specs=placed, out_specs=(P("grp", "shard", None), P()), check_vma=False
    )
```
